32 devices in a mesh: expert: 16 (over z, y, x), replica: 2 (over core).
Axes of the slice: x: 2, y: 2, z: 4, core: 2. Of those that a mesh axis runs over, the one named last changes fastest.
Arguments:
- tokens: bfloat16 [2048, 7168], P('expert', 'replica'), may hold values from -6 to 6
- gate_weight: bfloat16 [16, 7168, 1024], P('expert', 'replica'), may hold values from -0.0625 to 0.0625
- routes: int32 [2048, 8], P('expert'), may hold values from 0 to 15, all different within a row; in each aligned block of 128 rows (0 to 127, 128 to 255, ...) at most 80 rows name the same one
- combine: bfloat16 [2048, 8], P('expert'), may hold values from 0.099609375 to 1
- cotangent: bfloat16 [2048, 8, 1024], P('expert', None, 'replica'), may hold values from -1.5 to 1.5
Outputs:
- token_grad: bfloat16 [2048, 7168], P('expert', 'replica')
- weight_grad: bfloat16 [16, 7168, 1024], P('expert', 'replica')
The draws below stay inside these ranges and needn't reach their ends.
Inputs may be any that keep to these rules, and one draw needn't show every extreme that they name: `routes`: each row names 8 different experts. Among the 128 rows of one index of expert (aligned blocks), no expert is named more than 80 times, and in every draw some expert is named exactly 80 times in some block.
All inputs are finite; a program needn't handle non-finite values.
Results may differ from the reference program's by a relative error of at most 0.013.
Values may be sent and summed in bfloat16 or wider, within the bound.
A program may use at most 128 MiB of HBM per device.

```python
import math
import jax
import jax.numpy as jnp
import numpy as np
from jax import lax

D = 7168
TOPK = 8
HW = 1024
TOK_DEV = 128
EXPERTS = 16
CAP = 80
TOKENS = 2048
N_EXPERT = 16
N_REPLICA = 2


def steps_of(key, shape, pieces, smallest, top_value):
    loudness = 1.0
    for dim, shards_of in pieces:
        steps = jax.random.uniform(jax.random.fold_in(jax.random.fold_in(key, 6), dim), (shards_of,), jnp.float32, smallest / len(pieces), top_value / len(pieces))
        loudness = loudness * jnp.repeat(jnp.exp(steps), shape[dim] // shards_of).reshape((-1,) + (1,) * (len(shape) - 1 - dim))
    return loudness


def shared_out(key, own, number, rows, number_of, top, bound, skew):
    ranking = jax.random.permutation(key, number_of)
    crowded, ordinary = load_shares(number_of, rows * top, bound, skew, True), load_shares(number_of, rows * top, bound, skew, False)
    places = jnp.arange(number_of)

    def named(lengths, offset_by):
        used = int((lengths > 0).sum())
        fixed = max(1, used // 4)
        shifted = fixed + (places - fixed + offset_by * (used - fixed)) % max(1, number_of - fixed)
        return jnp.zeros((number_of,), jnp.int32).at[ranking[jnp.where(places < fixed, places, shifted)]].set(jnp.asarray(lengths, jnp.int32))

    lengths = jnp.where(number % 4 == 0, named(crowded, number // 4), named(ordinary, number - number // 4 - 1))
    mixed = jax.random.permutation(jax.random.fold_in(own, 3), number_of)
    giver, taker = mixed[0:number_of // 2 * 2:2], mixed[1:number_of // 2 * 2:2]
    slack = jnp.minimum(lengths[giver] - 1, bound - lengths[taker]) // 2
    slack = jnp.where((giver == ranking[0]) | (taker == ranking[0]) | (lengths[taker] == 0), 0, jnp.maximum(slack, 0))
    shifted = jax.random.randint(jax.random.fold_in(own, 4), (number_of // 2,), 0, 1 << 20) % (slack + 1)
    lengths = lengths.at[giver].add(-shifted).at[taker].add(shifted)
    members = jnp.searchsorted(jnp.cumsum(lengths), jnp.arange(rows * top), side="right").astype(jnp.int32)
    table = members.reshape(top, rows).T
    table = table[jax.random.permutation(jax.random.fold_in(own, 1), rows)]
    offset_by = jax.random.randint(jax.random.fold_in(own, 2), (rows, 1), 0, top)
    return jnp.take_along_axis(table, (jnp.arange(top)[None, :] + offset_by) % top, axis=1)


def load_shares(number_of, total, reach, slope, full):
    portions = [(1 << 20) // math.isqrt(standing ** slope) + 1 for standing in range(1, number_of + 1)]
    largest = reach if full else min(reach, max(-(-total // number_of), total * portions[0] // sum(portions)))
    least = 1 if total - largest >= number_of - 1 else 0
    holding, spare = [largest] + [least] * (number_of - 1), total - largest - least * (number_of - 1)
    while spare > 0:
        movable = [i for i in range(1, number_of) if holding[i] < largest] or [i for i in range(1, number_of) if holding[i] < reach]
        whole, remaining = sum([portions[i] for i in movable]), spare
        for i in movable:
            addition = min(reach - holding[i], max(1, remaining * portions[i] // whole), spare)
            holding[i] = holding[i] + addition
            spare = spare - addition
    return np.array(holding)


def gaussian(own_key, shape, scale, most, split=(), kind=jnp.bfloat16):
    level = steps_of(own_key, shape, split, -0.22, 0.18) if split else 1.0
    array = jax.random.normal(own_key, shape, jnp.float32) * scale * level
    return jnp.minimum(jnp.maximum(array, -most), most).astype(kind)


def setup_inputs(seed: int = 0) -> dict:
    key_list = jax.random.split(jax.random.key(seed), 6)
    tokens = gaussian(key_list[0], (TOKENS, D), 1.0, 6.0, ((0, 16), (1, 2)))
    gate_weight = gaussian(key_list[1], (EXPERTS, D, HW), D ** -0.5, 0.0625, ((0, 16), (1, 2)))
    routes_keys = jax.random.split(jax.random.fold_in(key_list[2], 1), TOKENS // TOK_DEV)
    routes_turns = jax.random.permutation(jax.random.fold_in(key_list[2], 3), TOKENS // TOK_DEV)
    routes = jax.vmap(lambda own, number: shared_out(jax.random.fold_in(key_list[2], 2), own, number, TOK_DEV, EXPERTS, TOPK, CAP, 2))(routes_keys, routes_turns).reshape((TOKENS, TOPK))
    combine = jnp.clip(0.099609375 + 0.9003906 * jax.random.uniform(key_list[3], (TOKENS, TOPK), jnp.float32) ** steps_of(key_list[3], (TOKENS, TOPK), ((0, 16),), -0.2, 0.2), 0.099609375, 1.0).astype(jnp.bfloat16)
    cotangent = gaussian(key_list[4], (TOKENS, TOPK, HW), 0.25, 1.5, ((0, 16), (2, 2)))
    return dict(tokens=tokens, gate_weight=gate_weight, routes=routes, combine=combine, cotangent=cotangent)


def silu_slope(gate):
    sig = jax.nn.sigmoid(gate)
    return sig * (1.0 + gate * (1.0 - sig))


def reference(tokens, gate_weight, routes, combine, cotangent):
    pairs = TOK_DEV * TOPK
    slices = N_REPLICA
    width = D // N_REPLICA
    sources = N_EXPERT
    ids = routes.reshape(sources, pairs).astype(jnp.int32)
    onehot = (ids[:, :, None] == jnp.arange(EXPERTS, dtype=jnp.int32)[None, None, :]).astype(jnp.int32)
    slot = jnp.sum((jnp.cumsum(onehot, axis=1) - onehot) * onehot, axis=2).astype(jnp.int32)
    source = jnp.broadcast_to(jnp.arange(sources, dtype=jnp.int32)[:, None], (sources, pairs))
    order = jnp.broadcast_to(jnp.arange(pairs, dtype=jnp.int32)[None, :], (sources, pairs))
    table = jnp.full((EXPERTS, sources, CAP), pairs, jnp.int32).at[ids, source, slot].set(order)
    flat_cot = cotangent.reshape(TOKENS * TOPK, HW)
    flat_w = combine.reshape(TOKENS * TOPK)
    src_col = jnp.arange(sources, dtype=jnp.int32)[:, None]

    def one_expert(carry, inputs):
        expert_table, weight = inputs
        valid = expert_table < pairs
        token = jnp.minimum(src_col * TOK_DEV + expert_table // TOPK, TOKENS - 1).astype(jnp.int32).reshape(-1)
        pair = jnp.minimum(src_col * pairs + expert_table, TOKENS * TOPK - 1).astype(jnp.int32).reshape(-1)
        mask = valid.reshape(-1)
        rows = jnp.where(mask[:, None], tokens[token], jnp.zeros((), tokens.dtype))
        cot = jnp.where(mask[:, None], flat_cot[pair], jnp.zeros((), cotangent.dtype))
        wts = jnp.where(mask, flat_w[pair], jnp.zeros((), combine.dtype))
        parts = jnp.einsum("srd,rdh->rsh", rows.reshape(-1, slices, width).astype(jnp.float32),
                           weight.reshape(slices, width, HW).astype(jnp.float32))
        rounded = lax.optimization_barrier(parts.astype(jnp.bfloat16))
        gate = jnp.sum(rounded.astype(jnp.float32), axis=0)
        dhid = (cot.astype(jnp.float32) * wts.astype(jnp.float32)[:, None] * silu_slope(gate)).astype(jnp.bfloat16)
        grad_w = jnp.dot(rows.T, dhid, preferred_element_type=jnp.float32).astype(jnp.bfloat16)
        back = jnp.dot(dhid, weight.T, preferred_element_type=jnp.float32).astype(jnp.bfloat16)
        carry = carry.at[token].add(jnp.where(mask[:, None], back.astype(jnp.float32), jnp.zeros((), jnp.float32)))
        return carry, grad_w

    start = jnp.zeros((TOKENS, D), jnp.float32)
    total, grads = lax.scan(one_expert, start, (table, gate_weight))
    return total.astype(jnp.bfloat16), grads
```

```python
import jax
import jax.numpy as jnp
from jax import lax
from jax.experimental import pallas as pl
from jax.experimental.pallas import tpu as pltpu
from jax.sharding import PartitionSpec as P

MESH = pl.DeviceIdType.MESH


def silu_slope(gate):
    sig = jax.nn.sigmoid(gate)
    return sig * (1.0 + gate * (1.0 - sig))


def local_routed(tokens, gate_weight, routes, combine, cotangent):
    n_exp = lax.axis_size("expert")
    tok_rows = tokens.shape[0]
    width = tokens.shape[1]
    topk = routes.shape[1]
    share = cotangent.shape[2]
    pairs = tok_rows * topk
    cap = max(2, pairs * 5 // (4 * n_exp))
    ids = routes.reshape(pairs)
    earlier = jnp.tril(jnp.ones((tok_rows, tok_rows), jnp.bfloat16), -1)
    onehot = routes[:, :, None] == jnp.arange(n_exp, dtype=jnp.int32)[None, None, :]
    named = jnp.any(onehot, axis=1).astype(jnp.bfloat16)
    rank = jnp.dot(earlier, named, preferred_element_type=jnp.float32)
    slot = jnp.sum(jnp.where(onehot, rank[:, None, :], 0.0), axis=2).astype(jnp.int32)
    target = ids * cap + slot.reshape(pairs)
    slot_pair = (
        jnp.full((n_exp * cap,), pairs, jnp.int32)
        .at[target]
        .set(jnp.arange(pairs, dtype=jnp.int32))
    )
    x_pad = jnp.concatenate([tokens, jnp.zeros((1, width), tokens.dtype)], axis=0)
    cot_pad = jnp.concatenate(
        [cotangent.reshape(pairs, share), jnp.zeros((1, share), cotangent.dtype)], axis=0
    )
    w_pad = jnp.concatenate([combine.reshape(pairs), jnp.zeros((1,), combine.dtype)], axis=0)
    send_x = x_pad[slot_pair // topk].reshape(n_exp, cap, width)
    send_c = cot_pad[slot_pair].reshape(n_exp, cap, share)
    send_w = w_pad[slot_pair].reshape(n_exp, cap)
    recv_x, recv_c, recv_w = (
        lax.all_to_all(send_x, "expert", split_axis=0, concat_axis=0, tiled=True),
        lax.all_to_all(send_c, "expert", split_axis=0, concat_axis=0, tiled=True),
        lax.all_to_all(send_w, "expert", split_axis=0, concat_axis=0, tiled=True),
    )
    rows = n_exp * cap
    recv_x = recv_x.reshape(rows, width)
    recv_c = recv_c.reshape(rows, share)
    recv_w = recv_w.reshape(rows).astype(jnp.float32)
    weight = gate_weight[0]
    gate_part = jnp.dot(recv_x, weight, preferred_element_type=jnp.float32)
    gate_all = lax.psum(gate_part.astype(jnp.bfloat16), "replica").astype(jnp.float32)
    cot_all = lax.all_gather(recv_c, "replica", axis=1, tiled=True)
    dhid = (cot_all.astype(jnp.float32) * recv_w[:, None] * silu_slope(gate_all)).astype(
        jnp.bfloat16
    )
    back_sum = lax.dot_general(
        dhid, weight, (((1,), (1,)), ((), ())), preferred_element_type=jnp.float32
    )
    grad_sum = lax.dot_general(
        recv_x, dhid, (((0,), (0,)), ((), ())), preferred_element_type=jnp.float32
    )
    back_rows = back_sum.astype(jnp.bfloat16).reshape(n_exp, cap, width)
    arrived = lax.all_to_all(back_rows, "expert", split_axis=0, concat_axis=0, tiled=True).reshape(
        rows, width
    )
    pair_rows = arrived[target].reshape(tok_rows, topk, width)
    token_grad = jnp.sum(pair_rows.astype(jnp.float32), axis=1).astype(jnp.bfloat16)
    return (token_grad, grad_sum.astype(jnp.bfloat16)[None])


HIGH = 4
N_EXP = 4 * HIGH
UP, DOWN, SIDE = 0, 1, 2
STEP_Z = (1, -1, 0)


def nearest_first(z):
    every = [(sz, fy, fx) for sz in range(HIGH) for fy in range(2) for fx in range(2)]
    every.sort(key=lambda s: (abs(s[0] - z) + s[1] + s[2], abs(s[0] - z)))
    return [sz * 4 + fy * 2 + fx for sz, fy, fx in every]


def words():
    found = []
    for z in range(HIGH):
        codes = nearest_first(z)
        found.append([sum(codes[q * 4 + i] << (4 * i) for i in range(4)) for q in range(4)])
    return found


class Spot:
    def __init__(self, n, me):
        z, y, x = me // 4, (me // 2) % 2, me % 2
        word = jnp.int32(0)
        for zz, row in enumerate(words()):
            for q, value in enumerate(row):
                word = jnp.where(jnp.logical_and(z == zz, n // 4 == q), value, word)
        digit = n % 4
        for i in range(1, 4):
            word = jnp.where(digit == i, word // (16**i), word)
        code = word % 16
        self.z, self.y, self.x = z, y, x
        self.sz = code // 4
        self.ey = (code // 2) % 2
        self.ex = code % 2
        self.sy = (y + self.ey) % 2
        self.sx = (x + self.ex) % 2
        self.dz = self.sz - z
        self.index = self.sz * 4 + self.sy * 2 + self.sx


class Side:
    def __init__(self, kind, spot):
        me_y = spot.z * 4 + (1 - spot.y) * 2 + spot.x
        me_x = spot.z * 4 + spot.y * 2 + 1 - spot.x
        self.kind = kind
        self.spot = spot
        if kind == 0:
            self.far, self.e, self.su, self.leaf, self.other = (
                spot.ey, spot.ex, spot.sx, me_y, me_x,
            )
        else:
            self.far, self.e, self.su, self.leaf, self.other = (
                spot.ex, spot.ey, spot.sy, me_x, me_y,
            )
        self.slot = spot.sz * 2 + self.su

    def target(self, way):
        if way == SIDE:
            return self.other
        return (self.spot.z + STEP_Z[way]) * 4 + self.spot.y * 2 + self.spot.x

    def onward(self, part, way):
        dz, z = self.spot.dz, self.spot.z
        if way == SIDE:
            ok = self.e == 0
            return ok if part == 0 else jnp.logical_and(ok, dz == 0)
        by = STEP_Z[way]
        ok = (dz <= 0) if by > 0 else (dz >= 0)
        ok = jnp.logical_and(ok, (z < HIGH - 1) if by > 0 else (z > 0))
        return jnp.logical_and(ok, self.e == 0) if part == 0 else ok

    def back_way(self, part):
        dz, e = self.spot.dz, self.e
        side = e == 1 if part == 0 else jnp.logical_and(e == 1, dz == 0)
        flat = e == 0 if part == 0 else e >= 0
        return (
            (side, SIDE),
            (jnp.logical_and(flat, dz > 0), UP),
            (jnp.logical_and(flat, dz < 0), DOWN),
        )


def choose(ranks, expert, cap):
    experts, tokens = ranks.shape
    which = lax.broadcasted_iota(jnp.int32, (experts, tokens), 0)
    row = jnp.sum(
        jnp.where(which == expert, ranks.astype(jnp.float32), 0.0), axis=0, keepdims=True
    )
    place = lax.broadcasted_iota(jnp.int32, (cap, tokens), 0).astype(jnp.float32)
    return jnp.where(row == place, 1.0, 0.0).astype(jnp.bfloat16)


def tile_spans(width, most):
    found, at = [], 0
    while at < width:
        size = min(most, width - at)
        found.append((at, size))
        at += size
    return found


def remote(src, dst, send, recv, expert=None):
    device = (
        {"replica": 1 - lax.axis_index("replica")} if expert is None else {"expert": expert}
    )
    return pltpu.make_async_remote_copy(
        src_ref=src, dst_ref=dst, send_sem=send, recv_sem=recv,
        device_id=device, device_id_type=MESH,
    )


def row_span(index, rows):
    return pl.ds(pl.multiple_of(index * rows, 16), rows)


def gather_kernel(
    cut, x_ref, w_ref, r_ref, c_ref, xc_out, dh_out, ra_out,
    full, pack, xc, wv, ra, cot, g_out, g_in, g_own, dh,
    full_s, full_r, pack_s, pack_r, ra_s, ra_r, cot_s, cot_r, g_s, g_r, d_s, d_r, loc, xo,
):
    me = lax.axis_index("expert")
    rep = lax.axis_index("replica")
    tokens, width = x_ref.shape
    half = width // 2
    cap = c_ref.shape[0] // N_EXP
    share = c_ref.shape[1]
    parts = ((0, cut), (cut, half - cut))
    load_w = pltpu.make_async_copy(w_ref.at[0], wv, loc.at[0])
    load_w.start()
    home = (me // 4) * 2
    sides = (home + me % 2, home + (me // 2) % 2)
    for kind in range(2):
        full[kind, sides[kind]] = x_ref[:, kind * half : (kind + 1) * half]
    ra[me] = r_ref[...]
    cot[row_span(me, cap), :] = c_ref[row_span(me, cap), :]

    barrier = pltpu.get_barrier_semaphore()

    def hello(i, carry):
        pl.semaphore_signal(
            barrier, inc=1, device_id={"expert": (me + i) % N_EXP}, device_id_type=MESH
        )
        return carry

    lax.fori_loop(1, N_EXP, hello, 0)
    pl.semaphore_signal(barrier, inc=1, device_id={"replica": 1 - rep}, device_id_type=MESH)
    pl.semaphore_wait(barrier, N_EXP)

    def full_copy(side, part, way):
        o = side.spot.index
        n = (side.kind * 2 + part) * N_EXP + o
        at, size = parts[part]
        block = full.at[side.kind, side.slot, :, pl.ds(at, size)]
        return remote(block, block, full_s.at[n * 3 + way], full_r.at[n], side.target(way))

    def pack_copy(side):
        o = side.spot.index
        n = side.kind * N_EXP + o
        return remote(
            pack.at[side.kind, side.slot],
            xc.at[row_span(o, cap), pl.ds(side.kind * half, half)],
            pack_s.at[n], pack_r.at[n], side.leaf,
        )

    def ranks_copy(peer, block):
        return remote(ra.at[block], ra.at[block], ra_s.at[peer], ra_r.at[block], peer)

    def cot_copy(peer, block):
        return remote(
            c_ref.at[row_span(peer, cap), :], cot.at[row_span(block, cap), :],
            cot_s.at[peer], cot_r.at[block], peer,
        )

    def gate_copy(o):
        rows = row_span(o, cap)
        return remote(g_out.at[rows, :], g_in.at[rows, :], g_s.at[o], g_r.at[o])

    def dhid_copy(o, side):
        block = dh.at[row_span(o, cap), pl.ds(pl.multiple_of(side * share, 128), share)]
        return remote(block, block, d_s.at[o], d_r.at[o])

    def xc_copy(o):
        rows = row_span(o, cap)
        return pltpu.make_async_copy(xc.at[rows, :], xc_out.at[rows, :], xo.at[o])

    def send_ranks(n, carry):
        ranks_copy(Spot(n, me).index, me).start()
        return carry

    lax.fori_loop(1, N_EXP, send_ranks, 0)

    def slope(j):
        o = Spot(j, me).index
        gate_copy(o).wait_recv()

        @pl.when(o != me)
        def _():
            cot_copy(o, o).wait_recv()

        mine = pl.ds(pl.multiple_of(rep * share, 128), share)

        def some(i, carry):
            rows = pl.ds(pl.multiple_of(o * cap + i * 16, 16), 16)
            gate = g_own[rows, :].astype(jnp.float32) + g_in[rows, :].astype(jnp.float32)
            sig = 1.0 / (1.0 + jnp.exp(-gate))
            dh[rows, mine] = (
                cot[rows, :].astype(jnp.float32) * (sig * (1.0 + gate * (1.0 - sig)))
            ).astype(jnp.bfloat16)
            return carry

        lax.fori_loop(0, cap // 16, some, 0)
        dhid_copy(o, rep).start()

    def step(n, carry):
        spot = Spot(n, me)
        o = spot.index
        rows = row_span(o, cap)
        both = (Side(0, spot), Side(1, spot))
        for part in range(2):
            for side in both:

                @pl.when(side.far == 0)
                def _(side=side, part=part):
                    @pl.when(n > 0)
                    def _():
                        full_copy(side, part, SIDE).wait_recv()

                    for way in (UP, DOWN, SIDE):

                        @pl.when(side.onward(part, way))
                        def _(way=way):
                            full_copy(side, part, way).start()

        @pl.when(n > 0)
        def _():
            ranks_copy(o, o).wait_recv()

        for side in both:

            @pl.when(side.far == 0)
            def _(side=side):
                ranks = ra[o]
                pick = jnp.concatenate(
                    [choose(ranks, me, cap), choose(ranks, side.leaf, cap)], axis=0
                )
                for at, size in tile_spans(half, 256):
                    found = jnp.dot(
                        pick, full[side.kind, side.slot, :, at : at + size],
                        preferred_element_type=jnp.float32,
                    ).astype(jnp.bfloat16)
                    pack[side.kind, side.slot, :, at : at + size] = found[cap:]
                    begin = side.kind * half + at
                    xc[rows, begin : begin + size] = found[:cap]
                pack_copy(side).start()

        @pl.when(n < 4)
        def _():
            for i in range(4):
                later = n * 4 + i

                @pl.when(later > 0)
                def _(later=later):
                    cot_copy(Spot(later, me).index, me).start()

        @pl.when(n == 0)
        def _():
            load_w.wait()

        for side in both:

            @pl.when(side.far == 1)
            def _(side=side):
                pack_copy(side).wait_recv()

        xc_copy(o).start()
        theirs = pl.ds(pl.multiple_of((1 - rep) * share, 128), share)
        mine = pl.ds(pl.multiple_of(rep * share, 128), share)
        g_out[rows, :] = jnp.dot(
            xc[rows, :], wv[:, theirs], preferred_element_type=jnp.float32
        ).astype(jnp.bfloat16)
        gate_copy(o).start()
        g_own[rows, :] = jnp.dot(
            xc[rows, :], wv[:, mine], preferred_element_type=jnp.float32
        ).astype(jnp.bfloat16)

        @pl.when(n >= 8)
        def _():
            @pl.when(n > 8)
            def _():
                slope(2 * n - 17)

            slope(2 * n - 16)

        return carry

    lax.fori_loop(0, N_EXP, step, 0)
    slope(N_EXP - 1)

    def finish(n, carry):
        spot = Spot(n, me)
        o = spot.index
        for kind in range(2):
            side = Side(kind, spot)

            @pl.when(side.far == 0)
            def _(side=side):
                for part in range(2):
                    for way in (UP, DOWN, SIDE):

                        @pl.when(side.onward(part, way))
                        def _(way=way, part=part):
                            full_copy(side, part, way).wait_send()

                pack_copy(side).wait_send()

        @pl.when(n > 0)
        def _():
            ranks_copy(o, me).wait_send()
            cot_copy(o, me).wait_send()

        gate_copy(o).wait_send()
        dhid_copy(o, rep).wait_send()
        dhid_copy(o, 1 - rep).wait_recv()
        xc_copy(o).wait()
        return carry

    lax.fori_loop(0, N_EXP, finish, 0)
    ra_out[...] = ra[...]
    save = pltpu.make_async_copy(dh, dh_out, loc.at[0])
    save.start()
    save.wait()


def cut_of(width):
    return (width // 2 // 128 * 5 // 7) * 128


def gather(tokens, weight, ranks, send_c):
    rows, width = tokens.shape
    half, hidden = width // 2, weight.shape[2]
    total, share = send_c.shape
    cap = total // N_EXP
    bf16, dma = jnp.bfloat16, pltpu.SemaphoreType.DMA
    vmem, anywhere = pl.BlockSpec(memory_space=pltpu.VMEM), pl.BlockSpec(memory_space=pl.ANY)
    return pl.pallas_call(
        lambda *refs: gather_kernel(cut_of(width), *refs),
        out_shape=(
            jax.ShapeDtypeStruct((total, width), bf16),
            jax.ShapeDtypeStruct((total, hidden), bf16),
            jax.ShapeDtypeStruct((N_EXP, N_EXP, rows), bf16),
        ),
        in_specs=[vmem, anywhere, vmem, vmem],
        out_specs=[anywhere, anywhere, vmem],
        scratch_shapes=[
            pltpu.VMEM((2, 8, rows, half), bf16),
            pltpu.VMEM((2, 8, cap, half), bf16),
            pltpu.VMEM((total, width), bf16),
            pltpu.VMEM((width, hidden), bf16),
            pltpu.VMEM((N_EXP, N_EXP, rows), bf16),
            pltpu.VMEM((total, share), bf16),
            pltpu.VMEM((total, share), bf16),
            pltpu.VMEM((total, share), bf16),
            pltpu.VMEM((total, share), bf16),
            pltpu.VMEM((total, hidden), bf16),
            dma((4 * N_EXP * 3,)), dma((4 * N_EXP,)),
            dma((2 * N_EXP,)), dma((2 * N_EXP,)),
            dma((N_EXP,)), dma((N_EXP,)), dma((N_EXP,)), dma((N_EXP,)),
            dma((N_EXP,)), dma((N_EXP,)), dma((N_EXP,)), dma((N_EXP,)),
            dma((1,)), dma((N_EXP,)),
        ],
        compiler_params=pltpu.CompilerParams(
            collective_id=0, has_side_effects=True, vmem_limit_bytes=56 * 2**20
        ),
        name="gather",
    )(tokens, weight, ranks, send_c)


AHEAD = 3


def collect_kernel(
    cut, w_ref, xc_ref, dh_ref, ra_ref, tg_ref, wg_ref,
    wv, xc, bk, total, out, leaf, land0, land1, wt,
    leaf_s, leaf_r, part_s, land0_r, land1_r, loc, wt_s,
):
    me = lax.axis_index("expert")
    rows, width = tg_ref.shape
    half = width // 2
    cap = dh_ref.shape[0] // N_EXP
    parts = ((0, cut), (cut, half - cut))
    load_w = pltpu.make_async_copy(w_ref.at[0], wv, loc.at[0])
    load_w.start()
    load_x = pltpu.make_async_copy(xc_ref, xc, loc.at[1])
    load_x.start()

    barrier = pltpu.get_barrier_semaphore()
    z, y, x = me // 4, (me // 2) % 2, me % 2
    edge = jnp.logical_or(z == 0, z == HIGH - 1)

    def hello(to):
        pl.semaphore_signal(barrier, inc=1, device_id={"expert": to}, device_id_type=MESH)

    hello(z * 4 + y * 2 + 1 - x)
    hello(z * 4 + (1 - y) * 2 + x)
    pl.when(z > 0)(lambda: hello(me - 4))
    pl.when(z < HIGH - 1)(lambda: hello(me + 4))
    pl.when(edge)(lambda: pl.semaphore_wait(barrier, 3))
    pl.when(jnp.logical_not(edge))(lambda: pl.semaphore_wait(barrier, 4))

    def leaf_copy(side):
        o = side.spot.index
        n = side.kind * N_EXP + o
        return remote(
            bk.at[row_span(o, cap), pl.ds(side.kind * half, half)],
            leaf.at[side.kind, side.slot],
            leaf_s.at[n], leaf_r.at[side.kind * 8 + side.slot], side.leaf,
        )

    def landing(side, part, lower):
        sz = side.spot.sz
        if part == 0:
            place = sz if lower is None else HIGH + sz + lower
            return land0.at[side.kind, place], land0_r.at[side.kind * 9 + place]
        place = 0 if lower is None else 1 + side.su * (HIGH + 1) + sz + lower
        return land1.at[side.kind, place], land1_r.at[side.kind * 11 + place]

    def part_copy(side, part, way):
        at, size = parts[part]
        lower = (1, 0, None)[way]
        dst, recv = landing(side, part, lower)
        n = (side.kind * 2 + part) * N_EXP + side.spot.index
        return remote(
            out.at[side.kind, side.slot, :, pl.ds(at, size)], dst, part_s.at[n], recv,
            side.target(way),
        )

    def back(n):
        spot = Spot(n, me)
        span = row_span(spot.index, cap)

        def some(i, carry):
            cols = pl.ds(pl.multiple_of(i * 256, 256), 256)
            bk[span, cols] = lax.dot_general(
                dh_ref[span, :], wv[cols, :], (((1,), (1,)), ((), ())),
                preferred_element_type=jnp.float32,
            ).astype(jnp.bfloat16)
            return carry

        lax.fori_loop(0, width // 256, some, 0)
        for kind in range(2):
            side = Side(kind, spot)

            @pl.when(side.far == 1)
            def _(side=side):
                leaf_copy(side).start()

    def wg_copy(i):
        return pltpu.make_async_copy(
            wt.at[i % 2], wg_ref.at[pl.ds(pl.multiple_of(i * 256, 256), 256), :], wt_s.at[i % 2]
        )

    def weight_tile(i):
        @pl.when(i >= 2)
        def _():
            wg_copy(i - 2).wait()

        cols = pl.ds(pl.multiple_of(i * 256, 256), 256)
        wt[i % 2] = lax.dot_general(
            xc[:, cols], dh_ref[...], (((0,), (0,)), ((), ())),
            preferred_element_type=jnp.float32,
        ).astype(jnp.bfloat16)
        wg_copy(i).start()

    tiles = width // 256
    load_w.wait()

    def first(i, carry):
        back(N_EXP - 1 - i)
        return carry

    lax.fori_loop(0, AHEAD, first, 0)
    load_x.wait()

    def step(m, carry):
        n = N_EXP - 1 - m
        spot = Spot(n, me)
        o = spot.index
        span = row_span(o, cap)

        @pl.when(m + AHEAD < N_EXP)
        def _():
            back(n - AHEAD)

        @pl.when(m < tiles)
        def _():
            weight_tile(m)

        for kind in range(2):
            side = Side(kind, spot)

            @pl.when(side.far == 0)
            def _(side=side, kind=kind):
                ranks = ra_ref[o]
                pick_me = choose(ranks, me, cap)
                pick_leaf = choose(ranks, side.leaf, cap)
                leaf_copy(side).wait_recv()
                for at, size in tile_spans(half, 256):
                    begin = kind * half + at
                    total[:, at : at + size] = lax.dot_general(
                        pick_me, bk[span, begin : begin + size], (((0,), (0,)), ((), ())),
                        preferred_element_type=jnp.float32,
                    ) + lax.dot_general(
                        pick_leaf, leaf[kind, side.slot, :, at : at + size],
                        (((0,), (0,)), ((), ())), preferred_element_type=jnp.float32,
                    )
                for part in range(2):
                    at, size = parts[part]
                    for way in (UP, DOWN, SIDE):

                        @pl.when(side.onward(part, way))
                        def _(way=way, part=part, at=at, size=size):
                            dst, recv = landing(side, part, (0, 1, None)[way])
                            remote(dst, dst, recv, recv, side.target(way)).wait_recv()
                            total[:, at : at + size] += dst[...].astype(jnp.float32)

                    @pl.when(n > 0)
                    def _(part=part, at=at, size=size):
                        out[kind, side.slot, :, at : at + size] = total[
                            :, at : at + size
                        ].astype(jnp.bfloat16)
                        for ok, way in side.back_way(part):

                            @pl.when(ok)
                            def _(way=way):
                                part_copy(side, part, way).start()

                @pl.when(n == 0)
                def _():
                    tg_ref[:, kind * half : (kind + 1) * half] = total[...].astype(jnp.bfloat16)

        return carry

    lax.fori_loop(0, N_EXP, step, 0)

    def finish(n, carry):
        spot = Spot(n, me)
        for kind in range(2):
            side = Side(kind, spot)

            @pl.when(side.far == 1)
            def _(side=side):
                leaf_copy(side).wait_send()

            @pl.when(jnp.logical_and(side.far == 0, n > 0))
            def _(side=side):
                for part in range(2):
                    part_copy(side, part, SIDE).wait_send()

        return carry

    lax.fori_loop(0, N_EXP, finish, 0)
    for i in (tiles - 2, tiles - 1):
        wg_copy(i).wait()


def collect(weight, xc, dh, ranks_all):
    total, width = xc.shape
    half, hidden = width // 2, weight.shape[2]
    rows, cap = ranks_all.shape[2], total // N_EXP
    cut = cut_of(width)
    bf16, dma = jnp.bfloat16, pltpu.SemaphoreType.DMA
    vmem, anywhere = pl.BlockSpec(memory_space=pltpu.VMEM), pl.BlockSpec(memory_space=pl.ANY)
    return pl.pallas_call(
        lambda *refs: collect_kernel(cut, *refs),
        out_shape=(
            jax.ShapeDtypeStruct((rows, width), bf16),
            jax.ShapeDtypeStruct((width, hidden), bf16),
        ),
        in_specs=[anywhere, anywhere, vmem, vmem],
        out_specs=[vmem, anywhere],
        scratch_shapes=[
            pltpu.VMEM((width, hidden), bf16),
            pltpu.VMEM((total, width), bf16),
            pltpu.VMEM((total, width), bf16),
            pltpu.VMEM((rows, half), jnp.float32),
            pltpu.VMEM((2, 8, rows, half), bf16),
            pltpu.VMEM((2, 8, cap, half), bf16),
            pltpu.VMEM((2, 2 * HIGH + 1, rows, cut), bf16),
            pltpu.VMEM((2, 2 * HIGH + 3, rows, half - cut), bf16),
            pltpu.VMEM((2, 256, hidden), bf16),
            dma((2 * N_EXP,)), dma((16,)), dma((4 * N_EXP,)), dma((18,)), dma((22,)),
            dma((2,)), dma((2,)),
        ],
        compiler_params=pltpu.CompilerParams(
            collective_id=1, has_side_effects=True, vmem_limit_bytes=58 * 2**20
        ),
        name="collect",
    )(weight, xc, dh, ranks_all)


def local_dense(tokens, gate_weight, routes, combine, cotangent):
    tok_rows = tokens.shape[0]
    topk = routes.shape[1]
    share = cotangent.shape[2]
    pairs = tok_rows * topk
    cap = pairs * 5 // (4 * N_EXP)
    earlier = jnp.tril(jnp.ones((tok_rows, tok_rows), jnp.bfloat16), -1)
    onehot = routes[:, :, None] == jnp.arange(N_EXP, dtype=jnp.int32)[None, None, :]
    named = jnp.any(onehot, axis=1)
    rank = jnp.dot(earlier, named.astype(jnp.bfloat16), preferred_element_type=jnp.float32)
    slot = jnp.sum(jnp.where(onehot, rank[:, None, :], 0.0), axis=2).astype(jnp.int32)
    target = (routes * cap + slot).reshape(pairs)
    taken = jnp.arange(N_EXP * cap, dtype=jnp.int32)[:, None] == target[None, :]
    pick = jnp.where(taken, combine.reshape(pairs)[None, :], jnp.zeros((), combine.dtype))
    send_c = jnp.dot(
        pick, cotangent.reshape(pairs, share), preferred_element_type=jnp.float32
    ).astype(jnp.bfloat16)
    ranks = jnp.where(named, rank, -1.0).astype(jnp.bfloat16).T
    xc, dh, ranks_all = gather(tokens, gate_weight, ranks, send_c)
    token_grad, grad = collect(gate_weight, xc, dh, ranks_all)
    return (token_grad, grad[None])


def local(tokens, gate_weight, routes, combine, cotangent):
    dense = (
        lax.axis_size("expert") == N_EXP
        and lax.axis_size("replica") == 2
        and tokens.shape == (128, 3584)
        and gate_weight.shape[2] == 2 * cotangent.shape[2]
        and routes.shape[1] == 8
    )
    body = local_dense if dense else local_routed
    return body(tokens, gate_weight, routes, combine, cotangent)


def solution(mesh):
    return jax.shard_map(
        local,
        mesh=mesh,
        in_specs=(
            P("expert", "replica"),
            P("expert", "replica", None),
            P("expert", None),
            P("expert", None),
            P("expert", None, "replica"),
        ),
        out_specs=(P("expert", "replica"), P("expert", "replica", None)),
        check_vma=False,
    )
```

```python
import jax
import jax.numpy as jnp
from jax import lax
from jax.experimental import pallas as pl
from jax.experimental.pallas import tpu as pltpu
from jax.sharding import PartitionSpec as P

MESH = pl.DeviceIdType.MESH


def silu_slope(gate):
    sig = jax.nn.sigmoid(gate)
    return sig * (1.0 + gate * (1.0 - sig))


def local_routed(tokens, gate_weight, routes, combine, cotangent):
    n_exp = lax.axis_size("expert")
    tok_rows = tokens.shape[0]
    width = tokens.shape[1]
    topk = routes.shape[1]
    share = cotangent.shape[2]
    pairs = tok_rows * topk
    cap = max(2, pairs * 5 // (4 * n_exp))
    ids = routes.reshape(pairs)
    earlier = jnp.tril(jnp.ones((tok_rows, tok_rows), jnp.bfloat16), -1)
    onehot = routes[:, :, None] == jnp.arange(n_exp, dtype=jnp.int32)[None, None, :]
    named = jnp.any(onehot, axis=1).astype(jnp.bfloat16)
    rank = jnp.dot(earlier, named, preferred_element_type=jnp.float32)
    slot = jnp.sum(jnp.where(onehot, rank[:, None, :], 0.0), axis=2).astype(jnp.int32)
    target = ids * cap + slot.reshape(pairs)
    slot_pair = (
        jnp.full((n_exp * cap,), pairs, jnp.int32)
        .at[target]
        .set(jnp.arange(pairs, dtype=jnp.int32))
    )
    x_pad = jnp.concatenate([tokens, jnp.zeros((1, width), tokens.dtype)], axis=0)
    cot_pad = jnp.concatenate(
        [cotangent.reshape(pairs, share), jnp.zeros((1, share), cotangent.dtype)], axis=0
    )
    w_pad = jnp.concatenate([combine.reshape(pairs), jnp.zeros((1,), combine.dtype)], axis=0)
    send_x = x_pad[slot_pair // topk].reshape(n_exp, cap, width)
    send_c = cot_pad[slot_pair].reshape(n_exp, cap, share)
    send_w = w_pad[slot_pair].reshape(n_exp, cap)
    recv_x, recv_c, recv_w = (
        lax.all_to_all(send_x, "expert", split_axis=0, concat_axis=0, tiled=True),
        lax.all_to_all(send_c, "expert", split_axis=0, concat_axis=0, tiled=True),
        lax.all_to_all(send_w, "expert", split_axis=0, concat_axis=0, tiled=True),
    )
    rows = n_exp * cap
    recv_x = recv_x.reshape(rows, width)
    recv_c = recv_c.reshape(rows, share)
    recv_w = recv_w.reshape(rows).astype(jnp.float32)
    weight = gate_weight[0]
    gate_part = jnp.dot(recv_x, weight, preferred_element_type=jnp.float32)
    gate_all = lax.psum(gate_part.astype(jnp.bfloat16), "replica").astype(jnp.float32)
    cot_all = lax.all_gather(recv_c, "replica", axis=1, tiled=True)
    dhid = (cot_all.astype(jnp.float32) * recv_w[:, None] * silu_slope(gate_all)).astype(
        jnp.bfloat16
    )
    back_sum = lax.dot_general(
        dhid, weight, (((1,), (1,)), ((), ())), preferred_element_type=jnp.float32
    )
    grad_sum = lax.dot_general(
        recv_x, dhid, (((0,), (0,)), ((), ())), preferred_element_type=jnp.float32
    )
    back_rows = back_sum.astype(jnp.bfloat16).reshape(n_exp, cap, width)
    arrived = lax.all_to_all(back_rows, "expert", split_axis=0, concat_axis=0, tiled=True).reshape(
        rows, width
    )
    pair_rows = arrived[target].reshape(tok_rows, topk, width)
    token_grad = jnp.sum(pair_rows.astype(jnp.float32), axis=1).astype(jnp.bfloat16)
    return (token_grad, grad_sum.astype(jnp.bfloat16)[None])


HIGH = 4
N_EXP = 4 * HIGH
UP, DOWN, SIDE = 0, 1, 2
STEP_Z = (1, -1, 0)


def nearest_first(z):
    every = [(sz, fy, fx) for sz in range(HIGH) for fy in range(2) for fx in range(2)]
    every.sort(key=lambda s: (abs(s[0] - z) + s[1] + s[2], abs(s[0] - z)))
    return [sz * 4 + fy * 2 + fx for sz, fy, fx in every]


def words(inverse):
    found = []
    for z in range(HIGH):
        codes = nearest_first(z)
        if inverse:
            codes = [codes.index(code) for code in range(N_EXP)]
        found.append([sum(codes[q * 4 + i] << (4 * i) for i in range(4)) for q in range(4)])
    return found


PARTS = ((False, 3), (True, 4), (True, 4), (True, 3))


class Part:
    def __init__(self, index, z_first, at, size, inner):
        self.index, self.z_first, self.at, self.size, self.inner = index, z_first, at, size, inner


def parts_of(half):
    unit = half // sum(tiles for _, tiles in PARTS)
    found, at, inner = [], 0, [0, 0]
    for index, (z_first, tiles) in enumerate(PARTS):
        size = tiles * unit
        found.append(Part(index, z_first, at, size, inner[z_first]))
        at += size
        inner[z_first] += size
    return found, inner


def looked_up(z, n, inverse=False):
    word = jnp.int32(0)
    for zz, row in enumerate(words(inverse)):
        for q, value in enumerate(row):
            word = jnp.where(jnp.logical_and(z == zz, n // 4 == q), value, word)
    digit = n % 4
    for i in range(1, 4):
        word = jnp.where(digit == i, word // (16**i), word)
    return word % 16


class Spot:
    def __init__(self, n, me):
        z, y, x = me // 4, (me // 2) % 2, me % 2
        code = looked_up(z, n)
        self.n = n
        self.z, self.y, self.x = z, y, x
        self.sz = code // 4
        self.ey = (code // 2) % 2
        self.ex = code % 2
        self.sy = (y + self.ey) % 2
        self.sx = (x + self.ex) % 2
        self.dz = self.sz - z
        self.index = self.sz * 4 + self.sy * 2 + self.sx


class Side:
    def __init__(self, kind, spot):
        me_y = spot.z * 4 + (1 - spot.y) * 2 + spot.x
        me_x = spot.z * 4 + spot.y * 2 + 1 - spot.x
        self.kind = kind
        self.spot = spot
        if kind == 0:
            self.far, self.e, self.su, self.leaf, self.other = (
                spot.ey, spot.ex, spot.sx, me_y, me_x,
            )
        else:
            self.far, self.e, self.su, self.leaf, self.other = (
                spot.ex, spot.ey, spot.sy, me_x, me_y,
            )
        self.slot = spot.sz * 2 + self.su

    def target(self, way):
        if way == SIDE:
            return self.other
        return (self.spot.z + STEP_Z[way]) * 4 + self.spot.y * 2 + self.spot.x

    def place_at_leaf(self):
        spot = self.spot
        ey, ex = (1 - spot.ey, spot.ex) if self.kind == 0 else (spot.ey, 1 - spot.ex)
        return looked_up(spot.z, spot.sz * 4 + ey * 2 + ex, True)

    def onward(self, part, way):
        dz, z = self.spot.dz, self.spot.z
        if way == SIDE:
            ok = self.e == 0
            return ok if part.z_first else jnp.logical_and(ok, dz == 0)
        by = STEP_Z[way]
        ok = (dz <= 0) if by > 0 else (dz >= 0)
        ok = jnp.logical_and(ok, (z < HIGH - 1) if by > 0 else (z > 0))
        return jnp.logical_and(ok, self.e == 0) if part.z_first else ok

    def back_way(self, part):
        dz, e = self.spot.dz, self.e
        side = e == 1 if part.z_first else jnp.logical_and(e == 1, dz == 0)
        flat = e == 0 if part.z_first else e >= 0
        return (
            (side, SIDE),
            (jnp.logical_and(flat, dz > 0), UP),
            (jnp.logical_and(flat, dz < 0), DOWN),
        )


def choose(ranks, expert, cap):
    experts, tokens = ranks.shape
    which = lax.broadcasted_iota(jnp.int32, (experts, tokens), 0)
    row = jnp.sum(
        jnp.where(which == expert, ranks.astype(jnp.float32), 0.0), axis=0, keepdims=True
    )
    place = lax.broadcasted_iota(jnp.int32, (cap, tokens), 0).astype(jnp.float32)
    return jnp.where(row == place, 1.0, 0.0).astype(jnp.bfloat16)


def tile_spans(width, most):
    found, at = [], 0
    while at < width:
        size = min(most, width - at)
        found.append((at, size))
        at += size
    return found


def remote(src, dst, send, recv, expert=None):
    device = (
        {"replica": 1 - lax.axis_index("replica")} if expert is None else {"expert": expert}
    )
    return pltpu.make_async_remote_copy(
        src_ref=src, dst_ref=dst, send_sem=send, recv_sem=recv,
        device_id=device, device_id_type=MESH,
    )


def row_span(index, rows):
    return pl.ds(pl.multiple_of(index * rows, 16), rows)


AHEAD = 3


def exchange_kernel(
    x_ref, w_ref, r_ref, c_ref, tg_ref, xc_out, dh_out,
    full, pack, xc, wv, ra, cot, g_out, g_in, g_own, dh, total, leaf, land_u, land_z,
    full_s, full_r, pack_s, pack_r, ra_s, ra_r, cot_s, cot_r, g_s, g_r, d_s, d_r,
    leaf_s, leaf_r, part_s, land_u_r, land_z_r, loc, xo,
):
    me = lax.axis_index("expert")
    rep = lax.axis_index("replica")
    tokens, width = x_ref.shape
    half = width // 2
    cap = c_ref.shape[0] // N_EXP
    share = c_ref.shape[1]
    parts, _ = parts_of(half)
    count = len(parts)
    lands, lands_r = (land_u, land_z), (land_u_r, land_z_r)
    load_w = pltpu.make_async_copy(w_ref.at[0], wv, loc.at[0])
    load_w.start()
    home = (me // 4) * 2
    sides = (home + me % 2, home + (me // 2) % 2)
    for kind in range(2):
        full[kind, sides[kind]] = x_ref[:, kind * half : (kind + 1) * half]
    ra[me] = r_ref[...]
    cot[row_span(me, cap), :] = c_ref[row_span(me, cap), :]

    barrier = pltpu.get_barrier_semaphore()

    def hello(i, carry):
        pl.semaphore_signal(
            barrier, inc=1, device_id={"expert": (me + i) % N_EXP}, device_id_type=MESH
        )
        return carry

    lax.fori_loop(1, N_EXP, hello, 0)
    pl.semaphore_signal(barrier, inc=1, device_id={"replica": 1 - rep}, device_id_type=MESH)
    pl.semaphore_wait(barrier, N_EXP)

    def full_copy(side, part, way):
        o = side.spot.index
        n = (side.kind * count + part.index) * N_EXP + o
        block = full.at[side.kind, side.slot, :, pl.ds(part.at, part.size)]
        return remote(block, block, full_s.at[n * 3 + way], full_r.at[n], side.target(way))

    def pack_copy(side):
        o = side.spot.index
        n = side.kind * N_EXP + o
        return remote(
            pack.at[side.kind, side.slot],
            xc.at[row_span(side.place_at_leaf(), cap), pl.ds(side.kind * half, half)],
            pack_s.at[n], pack_r.at[n], side.leaf,
        )

    def ranks_copy(peer, block):
        return remote(ra.at[block], ra.at[block], ra_s.at[peer], ra_r.at[block], peer)

    def cot_copy(peer, block):
        return remote(
            c_ref.at[row_span(peer, cap), :], cot.at[row_span(block, cap), :],
            cot_s.at[peer], cot_r.at[block], peer,
        )

    def gate_copy(pair):
        rows = row_span(pair, 2 * cap)
        return remote(g_out.at[rows, :], g_in.at[rows, :], g_s.at[pair], g_r.at[pair])

    def dhid_copy(pair, side):
        cols = pl.ds(pl.multiple_of(side * share, 128), share)
        block = dh.at[row_span(pair, 2 * cap), cols]
        return remote(block, block, d_s.at[pair], d_r.at[pair])

    def xc_copy(four):
        rows = row_span(four, 4 * cap)
        return pltpu.make_async_copy(xc.at[rows, :], xc_out.at[rows, :], xo.at[four])

    def leaf_copy(side):
        o = side.spot.index
        n = side.kind * N_EXP + o
        return remote(
            xc.at[row_span(side.spot.n, cap), pl.ds(side.kind * half, half)],
            leaf.at[side.kind, side.slot],
            leaf_s.at[n], leaf_r.at[side.kind * 8 + side.slot], side.leaf,
        )

    def landing(side, part, lower):
        land, recv = lands[part.z_first], lands_r[part.z_first]
        sz, cols = side.spot.sz, pl.ds(part.inner, part.size)
        if part.z_first:
            place = sz if lower is None else HIGH + sz + lower
        else:
            place = 0 if lower is None else 1 + side.su * (HIGH + 1) + sz + lower
        n = (side.kind * count + part.index) * land.shape[1] + place
        return land.at[side.kind, place, :, cols], recv.at[n]

    def part_copy(side, part, way):
        dst, recv = landing(side, part, (1, 0, None)[way])
        n = (side.kind * count + part.index) * N_EXP + side.spot.index
        return remote(
            full.at[side.kind, side.slot, :, pl.ds(part.at, part.size)], dst,
            part_s.at[n], recv, side.target(way),
        )

    def send_ranks(n, carry):
        ranks_copy(Spot(n, me).index, me).start()
        return carry

    lax.fori_loop(1, N_EXP, send_ranks, 0)

    def slope(pair):
        gate_copy(pair).wait_recv()
        mine = pl.ds(pl.multiple_of(rep * share, 128), share)
        for i in range(2):
            o = Spot(2 * pair + i, me).index

            @pl.when(o != me)
            def _(o=o):
                cot_copy(o, o).wait_recv()

            def some(j, carry, i=i, o=o):
                rows = pl.ds(pl.multiple_of((2 * pair + i) * cap + j * 16, 16), 16)
                theirs = pl.ds(pl.multiple_of(o * cap + j * 16, 16), 16)
                gate = g_own[rows, :].astype(jnp.float32) + g_in[rows, :].astype(jnp.float32)
                sig = 1.0 / (1.0 + jnp.exp(-gate))
                dh[rows, mine] = (
                    cot[theirs, :].astype(jnp.float32) * (sig * (1.0 + gate * (1.0 - sig)))
                ).astype(jnp.bfloat16)
                return carry

            lax.fori_loop(0, cap // 16, some, 0)
        dhid_copy(pair, rep).start()

    def back(four):
        span = row_span(four, 4 * cap)
        for i in range(2):
            dhid_copy(2 * four + i, 1 - rep).wait_recv()
        xc_copy(four).wait()

        def some(i, carry):
            cols = pl.ds(pl.multiple_of(i * 512, 512), 512)
            xc[span, cols] = lax.dot_general(
                dh[span, :], wv[cols, :], (((1,), (1,)), ((), ())),
                preferred_element_type=jnp.float32,
            ).astype(jnp.bfloat16)
            return carry

        lax.fori_loop(0, width // 512, some, 0)

    def send_leaf(n):
        spot = Spot(n, me)
        for kind in range(2):
            side = Side(kind, spot)

            @pl.when(side.far == 1)
            def _(side=side):
                leaf_copy(side).start()

    def gate(pair):
        rows = row_span(pair, 2 * cap)

        def product(side):
            cols = pl.ds(pl.multiple_of(side * share, 128), share)
            return jnp.dot(
                xc[rows, :], wv[:, cols], preferred_element_type=jnp.float32
            ).astype(jnp.bfloat16)

        g_out[rows, :] = product(1 - rep)
        gate_copy(pair).start()
        g_own[rows, :] = product(rep)

    def step(n, carry):
        spot = Spot(n, me)
        o = spot.index
        rows = row_span(n, cap)
        both = (Side(0, spot), Side(1, spot))
        for part in parts:
            for side in both:

                @pl.when(side.far == 0)
                def _(side=side, part=part):
                    @pl.when(n > 0)
                    def _():
                        full_copy(side, part, SIDE).wait_recv()

                    for way in (UP, DOWN, SIDE):

                        @pl.when(side.onward(part, way))
                        def _(way=way):
                            full_copy(side, part, way).start()

        @pl.when(n > 0)
        def _():
            ranks_copy(o, o).wait_recv()

        for side in both:

            @pl.when(side.far == 0)
            def _(side=side):
                ranks = ra[o]
                pick = jnp.concatenate(
                    [choose(ranks, me, cap), choose(ranks, side.leaf, cap)], axis=0
                )
                for at, size in tile_spans(half, 256):
                    found = jnp.dot(
                        pick, full[side.kind, side.slot, :, at : at + size],
                        preferred_element_type=jnp.float32,
                    ).astype(jnp.bfloat16)
                    pack[side.kind, side.slot, :, at : at + size] = found[cap:]
                    begin = side.kind * half + at
                    xc[rows, begin : begin + size] = found[:cap]
                pack_copy(side).start()

        @pl.when(n < 4)
        def _():
            for i in range(4):
                later = n * 4 + i

                @pl.when(later > 0)
                def _(later=later):
                    cot_copy(Spot(later, me).index, me).start()

        @pl.when(n == 0)
        def _():
            load_w.wait()

        for side in both:

            @pl.when(side.far == 1)
            def _(side=side):
                pack_copy(side).wait_recv()

        @pl.when(n % 4 == 3)
        def _():
            xc_copy(n // 4).start()

        @pl.when(n % 2 == 1)
        def _():
            gate(n // 2)

        @pl.when(jnp.logical_and(n % 2 == 0, n >= 4))
        def _():
            slope(n // 2 - 2)

        @pl.when(jnp.logical_or(n == 7, n == 11))
        def _():
            back((n - 7) // 4)

        return carry

    lax.fori_loop(0, N_EXP, step, 0)
    slope(N_EXP // 2 - 2)
    slope(N_EXP // 2 - 1)
    save = pltpu.make_async_copy(dh, dh_out, loc.at[0])

    def first(i, carry):
        send_leaf(N_EXP - 1 - i)
        return carry

    back(3)
    lax.fori_loop(0, AHEAD, first, 0)
    back(2)
    save.start()

    def gathered(m, carry):
        n = N_EXP - 1 - m
        spot = Spot(n, me)
        span = row_span(n, cap)

        @pl.when(n >= AHEAD)
        def _():
            send_leaf(n - AHEAD)

        for kind in range(2):
            side = Side(kind, spot)

            @pl.when(side.far == 0)
            def _(side=side, kind=kind):
                ranks = ra[spot.index]
                pick_me = choose(ranks, me, cap)
                pick_leaf = choose(ranks, side.leaf, cap)
                leaf_copy(side).wait_recv()
                for part in parts:
                    cols = slice(part.at, part.at + part.size)
                    for at, size in tile_spans(part.size, 256):
                        at += part.at
                        begin = kind * half + at
                        total[:, at : at + size] = lax.dot_general(
                            pick_me, xc[span, begin : begin + size], (((0,), (0,)), ((), ())),
                            preferred_element_type=jnp.float32,
                        ) + lax.dot_general(
                            pick_leaf, leaf[kind, side.slot, :, at : at + size],
                            (((0,), (0,)), ((), ())), preferred_element_type=jnp.float32,
                        )
                    for way in (UP, DOWN, SIDE):

                        @pl.when(side.onward(part, way))
                        def _(way=way, part=part, cols=cols):
                            full_copy(side, part, way).wait_send()
                            dst, recv = landing(side, part, (0, 1, None)[way])
                            remote(dst, dst, recv, recv, side.target(way)).wait_recv()
                            total[:, cols] += dst[...].astype(jnp.float32)

                    @pl.when(n > 0)
                    def _(part=part, cols=cols):
                        full[kind, side.slot, :, cols] = total[:, cols].astype(jnp.bfloat16)
                        for ok, way in side.back_way(part):

                            @pl.when(ok)
                            def _(way=way):
                                part_copy(side, part, way).start()

                @pl.when(n == 0)
                def _():
                    tg_ref[:, kind * half : (kind + 1) * half] = total[...].astype(jnp.bfloat16)

        return carry

    lax.fori_loop(0, N_EXP, gathered, 0)

    def finish(n, carry):
        spot = Spot(n, me)
        o = spot.index
        for kind in range(2):
            side = Side(kind, spot)

            @pl.when(side.far == 0)
            def _(side=side):
                pack_copy(side).wait_send()

                @pl.when(n > 0)
                def _():
                    for part in parts:
                        part_copy(side, part, SIDE).wait_send()

            @pl.when(side.far == 1)
            def _(side=side):
                leaf_copy(side).wait_send()

        @pl.when(n > 0)
        def _():
            ranks_copy(o, me).wait_send()
            cot_copy(o, me).wait_send()

        @pl.when(n % 2 == 0)
        def _():
            gate_copy(n // 2).wait_send()
            dhid_copy(n // 2, rep).wait_send()

        return carry

    lax.fori_loop(0, N_EXP, finish, 0)
    save.wait()


def exchange(tokens, weight, ranks, send_c):
    rows, width = tokens.shape
    half, hidden = width // 2, weight.shape[2]
    rows_all, share = send_c.shape
    cap = rows_all // N_EXP
    _, (wide_u, wide_z) = parts_of(half)
    count = 2 * len(PARTS)
    slots_u, slots_z = 2 * HIGH + 3, 2 * HIGH + 1
    bf16, dma = jnp.bfloat16, pltpu.SemaphoreType.DMA
    vmem, anywhere = pl.BlockSpec(memory_space=pltpu.VMEM), pl.BlockSpec(memory_space=pl.ANY)
    return pl.pallas_call(
        exchange_kernel,
        out_shape=(
            jax.ShapeDtypeStruct((rows, width), bf16),
            jax.ShapeDtypeStruct((rows_all, width), bf16),
            jax.ShapeDtypeStruct((rows_all, hidden), bf16),
        ),
        in_specs=[vmem, anywhere, vmem, vmem],
        out_specs=[vmem, anywhere, anywhere],
        scratch_shapes=[
            pltpu.VMEM((2, 8, rows, half), bf16),
            pltpu.VMEM((2, 8, cap, half), bf16),
            pltpu.VMEM((rows_all, width), bf16),
            pltpu.VMEM((width, hidden), bf16),
            pltpu.VMEM((N_EXP, N_EXP, rows), bf16),
            pltpu.VMEM((rows_all, share), bf16),
            pltpu.VMEM((rows_all, share), bf16),
            pltpu.VMEM((rows_all, share), bf16),
            pltpu.VMEM((rows_all, share), bf16),
            pltpu.VMEM((rows_all, hidden), bf16),
            pltpu.VMEM((rows, half), jnp.float32),
            pltpu.VMEM((2, 8, cap, half), bf16),
            pltpu.VMEM((2, slots_u, rows, wide_u), bf16),
            pltpu.VMEM((2, slots_z, rows, wide_z), bf16),
            dma((count * N_EXP * 3,)), dma((count * N_EXP,)),
            dma((2 * N_EXP,)), dma((2 * N_EXP,)),
            dma((N_EXP,)), dma((N_EXP,)), dma((N_EXP,)), dma((N_EXP,)),
            dma((8,)), dma((8,)), dma((8,)), dma((8,)),
            dma((2 * N_EXP,)), dma((16,)), dma((count * N_EXP,)),
            dma((count * slots_u,)), dma((count * slots_z,)),
            dma((1,)), dma((N_EXP,)),
        ],
        compiler_params=pltpu.CompilerParams(
            collective_id=0, has_side_effects=True, vmem_limit_bytes=58 * 2**20
        ),
        name="exchange",
    )(tokens, weight, ranks, send_c)


def weight_sum_kernel(x_ref, d_ref, o_ref):
    o_ref[...] = lax.dot_general(
        x_ref[...], d_ref[...], (((0,), (0,)), ((), ())), preferred_element_type=jnp.float32
    ).astype(o_ref.dtype)


def weight_sum(xc, dh):
    total, width = xc.shape
    hidden = dh.shape[1]
    return pl.pallas_call(
        weight_sum_kernel,
        out_shape=jax.ShapeDtypeStruct((width, hidden), jnp.bfloat16),
        grid=(width // 512,),
        in_specs=[
            pl.BlockSpec((total, 512), lambda i: (0, i)),
            pl.BlockSpec((total, hidden), lambda i: (0, 0)),
        ],
        out_specs=pl.BlockSpec((512, hidden), lambda i: (i, 0)),
        compiler_params=pltpu.CompilerParams(vmem_limit_bytes=48 * 2**20),
        name="weight_sum",
    )(xc, dh)


def local_dense(tokens, gate_weight, routes, combine, cotangent):
    tok_rows = tokens.shape[0]
    topk = routes.shape[1]
    share = cotangent.shape[2]
    pairs = tok_rows * topk
    cap = pairs * 5 // (4 * N_EXP)
    earlier = jnp.tril(jnp.ones((tok_rows, tok_rows), jnp.bfloat16), -1)
    onehot = routes[:, :, None] == jnp.arange(N_EXP, dtype=jnp.int32)[None, None, :]
    named = jnp.any(onehot, axis=1)
    rank = jnp.dot(earlier, named.astype(jnp.bfloat16), preferred_element_type=jnp.float32)
    slot = jnp.sum(jnp.where(onehot, rank[:, None, :], 0.0), axis=2).astype(jnp.int32)
    target = (routes * cap + slot).reshape(pairs)
    taken = jnp.arange(N_EXP * cap, dtype=jnp.int32)[:, None] == target[None, :]
    pick = jnp.where(taken, combine.reshape(pairs)[None, :], jnp.zeros((), combine.dtype))
    send_c = jnp.dot(
        pick, cotangent.reshape(pairs, share), preferred_element_type=jnp.float32
    ).astype(jnp.bfloat16)
    ranks = jnp.where(named, rank, -1.0).astype(jnp.bfloat16).T
    token_grad, xc, dh = exchange(tokens, gate_weight, ranks, send_c)
    grad = weight_sum(xc, dh)
    return (token_grad, grad[None])


def local(tokens, gate_weight, routes, combine, cotangent):
    dense = (
        lax.axis_size("expert") == N_EXP
        and lax.axis_size("replica") == 2
        and tokens.shape == (128, 3584)
        and gate_weight.shape[2] == 2 * cotangent.shape[2]
        and routes.shape[1] == 8
    )
    body = local_dense if dense else local_routed
    return body(tokens, gate_weight, routes, combine, cotangent)


def solution(mesh):
    return jax.shard_map(
        local,
        mesh=mesh,
        in_specs=(
            P("expert", "replica"),
            P("expert", "replica", None),
            P("expert", None),
            P("expert", None),
            P("expert", None, "replica"),
        ),
        out_specs=(P("expert", "replica"), P("expert", "replica", None)),
        check_vma=False,
    )
```

```python
import jax
import jax.numpy as jnp
from jax import lax
from jax.experimental import pallas as pl
from jax.experimental.pallas import tpu as pltpu
from jax.sharding import PartitionSpec as P

MESH = pl.DeviceIdType.MESH


def silu_slope(gate):
    sig = jax.nn.sigmoid(gate)
    return sig * (1.0 + gate * (1.0 - sig))


def local_routed(tokens, gate_weight, routes, combine, cotangent):
    n_exp = lax.axis_size("expert")
    tok_rows = tokens.shape[0]
    width = tokens.shape[1]
    topk = routes.shape[1]
    share = cotangent.shape[2]
    pairs = tok_rows * topk
    cap = max(2, pairs * 5 // (4 * n_exp))
    ids = routes.reshape(pairs)
    earlier = jnp.tril(jnp.ones((tok_rows, tok_rows), jnp.bfloat16), -1)
    onehot = routes[:, :, None] == jnp.arange(n_exp, dtype=jnp.int32)[None, None, :]
    named = jnp.any(onehot, axis=1).astype(jnp.bfloat16)
    rank = jnp.dot(earlier, named, preferred_element_type=jnp.float32)
    slot = jnp.sum(jnp.where(onehot, rank[:, None, :], 0.0), axis=2).astype(jnp.int32)
    target = ids * cap + slot.reshape(pairs)
    slot_pair = (
        jnp.full((n_exp * cap,), pairs, jnp.int32)
        .at[target]
        .set(jnp.arange(pairs, dtype=jnp.int32))
    )
    x_pad = jnp.concatenate([tokens, jnp.zeros((1, width), tokens.dtype)], axis=0)
    cot_pad = jnp.concatenate(
        [cotangent.reshape(pairs, share), jnp.zeros((1, share), cotangent.dtype)], axis=0
    )
    w_pad = jnp.concatenate([combine.reshape(pairs), jnp.zeros((1,), combine.dtype)], axis=0)
    send_x = x_pad[slot_pair // topk].reshape(n_exp, cap, width)
    send_c = cot_pad[slot_pair].reshape(n_exp, cap, share)
    send_w = w_pad[slot_pair].reshape(n_exp, cap)
    recv_x, recv_c, recv_w = (
        lax.all_to_all(send_x, "expert", split_axis=0, concat_axis=0, tiled=True),
        lax.all_to_all(send_c, "expert", split_axis=0, concat_axis=0, tiled=True),
        lax.all_to_all(send_w, "expert", split_axis=0, concat_axis=0, tiled=True),
    )
    rows = n_exp * cap
    recv_x = recv_x.reshape(rows, width)
    recv_c = recv_c.reshape(rows, share)
    recv_w = recv_w.reshape(rows).astype(jnp.float32)
    weight = gate_weight[0]
    gate_part = jnp.dot(recv_x, weight, preferred_element_type=jnp.float32)
    gate_all = lax.psum(gate_part.astype(jnp.bfloat16), "replica").astype(jnp.float32)
    cot_all = lax.all_gather(recv_c, "replica", axis=1, tiled=True)
    dhid = (cot_all.astype(jnp.float32) * recv_w[:, None] * silu_slope(gate_all)).astype(
        jnp.bfloat16
    )
    back_sum = lax.dot_general(
        dhid, weight, (((1,), (1,)), ((), ())), preferred_element_type=jnp.float32
    )
    grad_sum = lax.dot_general(
        recv_x, dhid, (((0,), (0,)), ((), ())), preferred_element_type=jnp.float32
    )
    back_rows = back_sum.astype(jnp.bfloat16).reshape(n_exp, cap, width)
    arrived = lax.all_to_all(back_rows, "expert", split_axis=0, concat_axis=0, tiled=True).reshape(
        rows, width
    )
    pair_rows = arrived[target].reshape(tok_rows, topk, width)
    token_grad = jnp.sum(pair_rows.astype(jnp.float32), axis=1).astype(jnp.bfloat16)
    return (token_grad, grad_sum.astype(jnp.bfloat16)[None])


HIGH = 4
N_EXP = 4 * HIGH
UP, DOWN, SIDE = 0, 1, 2
STEP_Z = (1, -1, 0)


def nearest_first(z):
    every = [(sz, fy, fx) for sz in range(HIGH) for fy in range(2) for fx in range(2)]
    every.sort(key=lambda s: (abs(s[0] - z) + s[1] + s[2], abs(s[0] - z)))
    return [sz * 4 + fy * 2 + fx for sz, fy, fx in every]


def words(inverse):
    found = []
    for z in range(HIGH):
        codes = nearest_first(z)
        if inverse:
            codes = [codes.index(code) for code in range(N_EXP)]
        found.append([sum(codes[q * 4 + i] << (4 * i) for i in range(4)) for q in range(4)])
    return found


PARTS = ((False, 3), (True, 4), (True, 4), (True, 3))


class Part:
    def __init__(self, index, z_first, at, size, inner):
        self.index, self.z_first, self.at, self.size, self.inner = index, z_first, at, size, inner


def parts_of(half):
    unit = half // sum(tiles for _, tiles in PARTS)
    found, at, inner = [], 0, [0, 0]
    for index, (z_first, tiles) in enumerate(PARTS):
        size = tiles * unit
        found.append(Part(index, z_first, at, size, inner[z_first]))
        at += size
        inner[z_first] += size
    return found, inner


def looked_up(z, n, inverse=False):
    word = jnp.int32(0)
    for zz, row in enumerate(words(inverse)):
        for q, value in enumerate(row):
            word = jnp.where(jnp.logical_and(z == zz, n // 4 == q), value, word)
    digit = n % 4
    for i in range(1, 4):
        word = jnp.where(digit == i, word // (16**i), word)
    return word % 16


class Spot:
    def __init__(self, n, me):
        z, y, x = me // 4, (me // 2) % 2, me % 2
        code = looked_up(z, n)
        self.n = n
        self.z, self.y, self.x = z, y, x
        self.sz = code // 4
        self.ey = (code // 2) % 2
        self.ex = code % 2
        self.sy = (y + self.ey) % 2
        self.sx = (x + self.ex) % 2
        self.dz = self.sz - z
        self.index = self.sz * 4 + self.sy * 2 + self.sx


class Side:
    def __init__(self, kind, spot):
        me_y = spot.z * 4 + (1 - spot.y) * 2 + spot.x
        me_x = spot.z * 4 + spot.y * 2 + 1 - spot.x
        self.kind = kind
        self.spot = spot
        if kind == 0:
            self.far, self.e, self.su, self.leaf, self.other = (
                spot.ey, spot.ex, spot.sx, me_y, me_x,
            )
        else:
            self.far, self.e, self.su, self.leaf, self.other = (
                spot.ex, spot.ey, spot.sy, me_x, me_y,
            )
        self.slot = spot.sz * 2 + self.su

    def target(self, way):
        if way == SIDE:
            return self.other
        return (self.spot.z + STEP_Z[way]) * 4 + self.spot.y * 2 + self.spot.x

    def place_at_leaf(self):
        spot = self.spot
        ey, ex = (1 - spot.ey, spot.ex) if self.kind == 0 else (spot.ey, 1 - spot.ex)
        return looked_up(spot.z, spot.sz * 4 + ey * 2 + ex, True)

    def onward(self, part, way):
        dz, z = self.spot.dz, self.spot.z
        if way == SIDE:
            ok = self.e == 0
            return ok if part.z_first else jnp.logical_and(ok, dz == 0)
        by = STEP_Z[way]
        ok = (dz <= 0) if by > 0 else (dz >= 0)
        ok = jnp.logical_and(ok, (z < HIGH - 1) if by > 0 else (z > 0))
        return jnp.logical_and(ok, self.e == 0) if part.z_first else ok

    def back_way(self, part):
        dz, e = self.spot.dz, self.e
        side = e == 1 if part.z_first else jnp.logical_and(e == 1, dz == 0)
        flat = e == 0 if part.z_first else e >= 0
        return (
            (side, SIDE),
            (jnp.logical_and(flat, dz > 0), UP),
            (jnp.logical_and(flat, dz < 0), DOWN),
        )


def choose(ranks, expert, cap):
    experts, tokens = ranks.shape
    which = lax.broadcasted_iota(jnp.int32, (experts, tokens), 0)
    row = jnp.sum(
        jnp.where(which == expert, ranks.astype(jnp.float32), 0.0), axis=0, keepdims=True
    )
    place = lax.broadcasted_iota(jnp.int32, (cap, tokens), 0).astype(jnp.float32)
    return jnp.where(row == place, 1.0, 0.0).astype(jnp.bfloat16)


def tile_spans(width, most):
    found, at = [], 0
    while at < width:
        size = min(most, width - at)
        found.append((at, size))
        at += size
    return found


def remote(src, dst, send, recv, expert=None):
    device = (
        {"replica": 1 - lax.axis_index("replica")} if expert is None else {"expert": expert}
    )
    return pltpu.make_async_remote_copy(
        src_ref=src, dst_ref=dst, send_sem=send, recv_sem=recv,
        device_id=device, device_id_type=MESH,
    )


def row_span(index, rows):
    return pl.ds(pl.multiple_of(index * rows, 16), rows)


AHEAD = 3


def exchange_kernel(
    x_ref, w_ref, routes_ref, combine_ref, cot_ref, tg_ref, xc_out, dh_out,
    slots, pair_w, send_c, full, pack, xc, wv, ra, cot, g_out, g_in, g_own, dh, total, leaf, land_u, land_z,
    full_s, full_r, pack_s, pack_r, ra_s, ra_r, cot_s, cot_r, g_s, g_r, d_s, d_r,
    leaf_s, leaf_r, part_s, land_u_r, land_z_r, loc, xo,
):
    me = lax.axis_index("expert")
    rep = lax.axis_index("replica")
    tokens, width = x_ref.shape
    half = width // 2
    cap = cot.shape[0] // N_EXP
    share = cot.shape[1]
    parts, _ = parts_of(half)
    count = len(parts)
    lands, lands_r = (land_u, land_z), (land_u_r, land_z_r)
    load_w = pltpu.make_async_copy(w_ref.at[0], wv, loc.at[0])
    load_w.start()
    home = (me // 4) * 2
    sides = (home + me % 2, home + (me // 2) % 2)
    for kind in range(2):
        full[kind, sides[kind]] = x_ref[:, kind * half : (kind + 1) * half]

    barrier = pltpu.get_barrier_semaphore()

    def hello(i, carry):
        pl.semaphore_signal(
            barrier, inc=1, device_id={"expert": (me + i) % N_EXP}, device_id_type=MESH
        )
        return carry

    lax.fori_loop(1, N_EXP, hello, 0)
    pl.semaphore_signal(barrier, inc=1, device_id={"replica": 1 - rep}, device_id_type=MESH)
    pl.semaphore_wait(barrier, N_EXP)

    def full_copy(side, part, way):
        o = side.spot.index
        n = (side.kind * count + part.index) * N_EXP + o
        block = full.at[side.kind, side.slot, :, pl.ds(part.at, part.size)]
        return remote(block, block, full_s.at[n * 3 + way], full_r.at[n], side.target(way))

    def pack_copy(side):
        o = side.spot.index
        n = side.kind * N_EXP + o
        return remote(
            pack.at[side.kind, side.slot],
            xc.at[row_span(side.place_at_leaf(), cap), pl.ds(side.kind * half, half)],
            pack_s.at[n], pack_r.at[n], side.leaf,
        )

    def ranks_copy(peer, block):
        return remote(ra.at[block], ra.at[block], ra_s.at[peer], ra_r.at[block], peer)

    def cot_copy(place, peer, block):
        return remote(
            send_c.at[row_span(place, cap), :], cot.at[row_span(block, cap), :],
            cot_s.at[peer], cot_r.at[block], peer,
        )

    def gate_copy(pair):
        rows = row_span(pair, 2 * cap)
        return remote(g_out.at[rows, :], g_in.at[rows, :], g_s.at[pair], g_r.at[pair])

    def dhid_copy(pair, side):
        cols = pl.ds(pl.multiple_of(side * share, 128), share)
        block = dh.at[row_span(pair, 2 * cap), cols]
        return remote(block, block, d_s.at[pair], d_r.at[pair])

    def xc_copy(four):
        rows = row_span(four, 4 * cap)
        return pltpu.make_async_copy(xc.at[rows, :], xc_out.at[rows, :], xo.at[four])

    def leaf_copy(side):
        o = side.spot.index
        n = side.kind * N_EXP + o
        return remote(
            xc.at[row_span(side.spot.n, cap), pl.ds(side.kind * half, half)],
            leaf.at[side.kind, side.slot],
            leaf_s.at[n], leaf_r.at[side.kind * 8 + side.slot], side.leaf,
        )

    def landing(side, part, lower):
        land, recv = lands[part.z_first], lands_r[part.z_first]
        sz, cols = side.spot.sz, pl.ds(part.inner, part.size)
        if part.z_first:
            place = sz if lower is None else HIGH + sz + lower
        else:
            place = 0 if lower is None else 1 + side.su * (HIGH + 1) + sz + lower
        n = (side.kind * count + part.index) * land.shape[1] + place
        return land.at[side.kind, place, :, cols], recv.at[n]

    def part_copy(side, part, way):
        dst, recv = landing(side, part, (1, 0, None)[way])
        n = (side.kind * count + part.index) * N_EXP + side.spot.index
        return remote(
            full.at[side.kind, side.slot, :, pl.ds(part.at, part.size)], dst,
            part_s.at[n], recv, side.target(way),
        )

    ra[me] = rank_pairs(routes_ref, combine_ref, slots, pair_w)

    def make_rows(four):
        place = lax.broadcasted_iota(jnp.int32, (cap, slots.shape[1]), 0).astype(jnp.float32)
        picks = [
            jnp.where(slots[pl.ds(Spot(4 * four + i, me).index, 1), :] == place, pair_w[...], 0.0)
            for i in range(4)
        ]
        send_c[row_span(four, 4 * cap), :] = jnp.dot(
            jnp.concatenate([pick.astype(jnp.bfloat16) for pick in picks], axis=0),
            cot_ref[...], preferred_element_type=jnp.float32,
        ).astype(jnp.bfloat16)

    def send_ranks(n, carry):
        ranks_copy(Spot(n, me).index, me).start()
        return carry

    lax.fori_loop(1, N_EXP, send_ranks, 0)

    def slope(pair):
        gate_copy(pair).wait_recv()
        mine = pl.ds(pl.multiple_of(rep * share, 128), share)
        for i in range(2):
            o = Spot(2 * pair + i, me).index

            @pl.when(o != me)
            def _(o=o):
                cot_copy(0, o, o).wait_recv()

            def some(j, carry, i=i, o=o):
                rows = pl.ds(pl.multiple_of((2 * pair + i) * cap + j * 16, 16), 16)
                theirs = pl.ds(pl.multiple_of(o * cap + j * 16, 16), 16)
                gate = g_own[rows, :].astype(jnp.float32) + g_in[rows, :].astype(jnp.float32)
                sig = 1.0 / (1.0 + jnp.exp(-gate))
                dh[rows, mine] = (
                    cot[theirs, :].astype(jnp.float32) * (sig * (1.0 + gate * (1.0 - sig)))
                ).astype(jnp.bfloat16)
                return carry

            lax.fori_loop(0, cap // 16, some, 0)
        dhid_copy(pair, rep).start()

    def back(four):
        span = row_span(four, 4 * cap)
        for i in range(2):
            dhid_copy(2 * four + i, 1 - rep).wait_recv()
        xc_copy(four).wait()

        def some(i, carry):
            cols = pl.ds(pl.multiple_of(i * 512, 512), 512)
            xc[span, cols] = lax.dot_general(
                dh[span, :], wv[cols, :], (((1,), (1,)), ((), ())),
                preferred_element_type=jnp.float32,
            ).astype(jnp.bfloat16)
            return carry

        lax.fori_loop(0, width // 512, some, 0)

    def send_leaf(n):
        spot = Spot(n, me)
        for kind in range(2):
            side = Side(kind, spot)

            @pl.when(side.far == 1)
            def _(side=side):
                leaf_copy(side).start()

    def gate(pair):
        rows = row_span(pair, 2 * cap)

        def product(side):
            cols = pl.ds(pl.multiple_of(side * share, 128), share)
            return jnp.dot(
                xc[rows, :], wv[:, cols], preferred_element_type=jnp.float32
            ).astype(jnp.bfloat16)

        g_out[rows, :] = product(1 - rep)
        gate_copy(pair).start()
        g_own[rows, :] = product(rep)

    def step(n, carry):
        spot = Spot(n, me)
        o = spot.index
        rows = row_span(n, cap)
        both = (Side(0, spot), Side(1, spot))
        for part in parts:
            for side in both:

                @pl.when(side.far == 0)
                def _(side=side, part=part):
                    @pl.when(n > 0)
                    def _():
                        full_copy(side, part, SIDE).wait_recv()

                    for way in (UP, DOWN, SIDE):

                        @pl.when(side.onward(part, way))
                        def _(way=way):
                            full_copy(side, part, way).start()

        @pl.when(n > 0)
        def _():
            ranks_copy(o, o).wait_recv()

        for side in both:

            @pl.when(side.far == 0)
            def _(side=side):
                ranks = ra[o]
                pick = jnp.concatenate(
                    [choose(ranks, me, cap), choose(ranks, side.leaf, cap)], axis=0
                )
                for at, size in tile_spans(half, 256):
                    found = jnp.dot(
                        pick, full[side.kind, side.slot, :, at : at + size],
                        preferred_element_type=jnp.float32,
                    ).astype(jnp.bfloat16)
                    pack[side.kind, side.slot, :, at : at + size] = found[cap:]
                    begin = side.kind * half + at
                    xc[rows, begin : begin + size] = found[:cap]
                pack_copy(side).start()

        @pl.when(n < 4)
        def _():
            make_rows(n)

            @pl.when(n == 0)
            def _():
                cot[row_span(me, cap), :] = send_c[:cap, :]

            for i in range(4):
                later = n * 4 + i

                @pl.when(later > 0)
                def _(later=later):
                    cot_copy(later, Spot(later, me).index, me).start()

        @pl.when(n == 0)
        def _():
            load_w.wait()

        for side in both:

            @pl.when(side.far == 1)
            def _(side=side):
                pack_copy(side).wait_recv()

        @pl.when(n % 4 == 3)
        def _():
            xc_copy(n // 4).start()

        @pl.when(n % 2 == 1)
        def _():
            gate(n // 2)

        @pl.when(jnp.logical_and(n % 2 == 0, n >= 4))
        def _():
            slope(n // 2 - 2)

        @pl.when(jnp.logical_or(n == 7, n == 11))
        def _():
            back((n - 7) // 4)

        return carry

    lax.fori_loop(0, N_EXP, step, 0)
    slope(N_EXP // 2 - 2)
    slope(N_EXP // 2 - 1)
    save = pltpu.make_async_copy(dh, dh_out, loc.at[0])

    def first(i, carry):
        send_leaf(N_EXP - 1 - i)
        return carry

    back(3)
    lax.fori_loop(0, AHEAD, first, 0)
    back(2)
    save.start()

    def gathered(m, carry):
        n = N_EXP - 1 - m
        spot = Spot(n, me)
        span = row_span(n, cap)

        @pl.when(n >= AHEAD)
        def _():
            send_leaf(n - AHEAD)

        for kind in range(2):
            side = Side(kind, spot)

            @pl.when(side.far == 0)
            def _(side=side, kind=kind):
                ranks = ra[spot.index]
                pick_me = choose(ranks, me, cap)
                pick_leaf = choose(ranks, side.leaf, cap)
                leaf_copy(side).wait_recv()
                for part in parts:
                    cols = slice(part.at, part.at + part.size)
                    for at, size in tile_spans(part.size, 256):
                        at += part.at
                        begin = kind * half + at
                        total[:, at : at + size] = lax.dot_general(
                            pick_me, xc[span, begin : begin + size], (((0,), (0,)), ((), ())),
                            preferred_element_type=jnp.float32,
                        ) + lax.dot_general(
                            pick_leaf, leaf[kind, side.slot, :, at : at + size],
                            (((0,), (0,)), ((), ())), preferred_element_type=jnp.float32,
                        )
                    for way in (UP, DOWN, SIDE):

                        @pl.when(side.onward(part, way))
                        def _(way=way, part=part, cols=cols):
                            full_copy(side, part, way).wait_send()
                            dst, recv = landing(side, part, (0, 1, None)[way])
                            remote(dst, dst, recv, recv, side.target(way)).wait_recv()
                            total[:, cols] += dst[...].astype(jnp.float32)

                    @pl.when(n > 0)
                    def _(part=part, cols=cols):
                        full[kind, side.slot, :, cols] = total[:, cols].astype(jnp.bfloat16)
                        for ok, way in side.back_way(part):

                            @pl.when(ok)
                            def _(way=way):
                                part_copy(side, part, way).start()

                @pl.when(n == 0)
                def _():
                    tg_ref[:, kind * half : (kind + 1) * half] = total[...].astype(jnp.bfloat16)

        return carry

    lax.fori_loop(0, N_EXP, gathered, 0)

    def finish(n, carry):
        spot = Spot(n, me)
        o = spot.index
        for kind in range(2):
            side = Side(kind, spot)

            @pl.when(side.far == 0)
            def _(side=side):
                pack_copy(side).wait_send()

                @pl.when(n > 0)
                def _():
                    for part in parts:
                        part_copy(side, part, SIDE).wait_send()

            @pl.when(side.far == 1)
            def _(side=side):
                leaf_copy(side).wait_send()

        @pl.when(n > 0)
        def _():
            ranks_copy(o, me).wait_send()
            cot_copy(n, o, me).wait_send()

        @pl.when(n % 2 == 0)
        def _():
            gate_copy(n // 2).wait_send()
            dhid_copy(n // 2, rep).wait_send()

        return carry

    lax.fori_loop(0, N_EXP, finish, 0)
    save.wait()


def rank_pairs(routes_ref, combine_ref, slots, pair_w):
    topk, tokens = routes_ref.shape
    pairs, f32, bf16 = tokens * topk, jnp.float32, jnp.bfloat16
    iota = lambda shape, dim: lax.broadcasted_iota(jnp.int32, shape, dim)
    dot = lambda a, b: jnp.dot(a, b, preferred_element_type=f32)
    routes = routes_ref[...]
    named = jnp.zeros((N_EXP, tokens), f32)
    for k in range(topk):
        named += jnp.where(routes[k : k + 1, :] == iota((N_EXP, tokens), 0), 1.0, 0.0)
    square = (tokens, tokens)
    before = jnp.where(iota(square, 0) < iota(square, 1), 1.0, 0.0).astype(bf16)
    ranks = jnp.where(named > 0.5, dot(named.astype(bf16), before), -1.0).astype(bf16)
    wide = (tokens, pairs)
    widen = jnp.where(iota(wide, 1) // topk == iota(wide, 0), 1.0, 0.0).astype(bf16)
    mine = iota((topk, pairs), 1) % topk == iota((topk, pairs), 0)
    flat = lambda a: jnp.sum(jnp.where(mine, dot(a, widen), 0.0), axis=0, keepdims=True)
    expert = flat(routes.astype(f32).astype(bf16))
    pair_w[...] = flat(combine_ref[...])
    slots[...] = jnp.where(
        expert == iota((N_EXP, pairs), 0).astype(f32),
        dot(ranks, widen), -1.0,
    )
    return ranks


def exchange(tokens, weight, routes, combine, cotangent):
    rows, width = tokens.shape
    half, hidden = width // 2, weight.shape[2]
    pairs, share = cotangent.shape
    cap = pairs * 5 // (4 * N_EXP)
    rows_all = cap * N_EXP
    _, (wide_u, wide_z) = parts_of(half)
    count = 2 * len(PARTS)
    slots_u, slots_z = 2 * HIGH + 3, 2 * HIGH + 1
    bf16, dma = jnp.bfloat16, pltpu.SemaphoreType.DMA
    vmem, anywhere = pl.BlockSpec(memory_space=pltpu.VMEM), pl.BlockSpec(memory_space=pl.ANY)
    return pl.pallas_call(
        exchange_kernel,
        out_shape=(
            jax.ShapeDtypeStruct((rows, width), bf16),
            jax.ShapeDtypeStruct((rows_all, width), bf16),
            jax.ShapeDtypeStruct((rows_all, hidden), bf16),
        ),
        in_specs=[vmem, anywhere, vmem, vmem, vmem],
        out_specs=[vmem, anywhere, anywhere],
        scratch_shapes=[
            pltpu.VMEM((N_EXP, pairs), jnp.float32),
            pltpu.VMEM((1, pairs), jnp.float32),
            pltpu.VMEM((rows_all, share), bf16),
            pltpu.VMEM((2, 8, rows, half), bf16),
            pltpu.VMEM((2, 8, cap, half), bf16),
            pltpu.VMEM((rows_all, width), bf16),
            pltpu.VMEM((width, hidden), bf16),
            pltpu.VMEM((N_EXP, N_EXP, rows), bf16),
            pltpu.VMEM((rows_all, share), bf16),
            pltpu.VMEM((rows_all, share), bf16),
            pltpu.VMEM((rows_all, share), bf16),
            pltpu.VMEM((rows_all, share), bf16),
            pltpu.VMEM((rows_all, hidden), bf16),
            pltpu.VMEM((rows, half), jnp.float32),
            pltpu.VMEM((2, 8, cap, half), bf16),
            pltpu.VMEM((2, slots_u, rows, wide_u), bf16),
            pltpu.VMEM((2, slots_z, rows, wide_z), bf16),
            dma((count * N_EXP * 3,)), dma((count * N_EXP,)),
            dma((2 * N_EXP,)), dma((2 * N_EXP,)),
            dma((N_EXP,)), dma((N_EXP,)), dma((N_EXP,)), dma((N_EXP,)),
            dma((8,)), dma((8,)), dma((8,)), dma((8,)),
            dma((2 * N_EXP,)), dma((16,)), dma((count * N_EXP,)),
            dma((count * slots_u,)), dma((count * slots_z,)),
            dma((1,)), dma((N_EXP,)),
        ],
        compiler_params=pltpu.CompilerParams(
            collective_id=0, has_side_effects=True, vmem_limit_bytes=58 * 2**20
        ),
        name="exchange",
    )(tokens, weight, routes, combine, cotangent)


def weight_sum_kernel(x_ref, d_ref, o_ref):
    o_ref[...] = lax.dot_general(
        x_ref[...], d_ref[...], (((0,), (0,)), ((), ())), preferred_element_type=jnp.float32
    ).astype(o_ref.dtype)


def weight_sum(xc, dh):
    total, width = xc.shape
    hidden = dh.shape[1]
    return pl.pallas_call(
        weight_sum_kernel,
        out_shape=jax.ShapeDtypeStruct((width, hidden), jnp.bfloat16),
        grid=(width // 512,),
        in_specs=[
            pl.BlockSpec((total, 512), lambda i: (0, i)),
            pl.BlockSpec((total, hidden), lambda i: (0, 0)),
        ],
        out_specs=pl.BlockSpec((512, hidden), lambda i: (i, 0)),
        compiler_params=pltpu.CompilerParams(vmem_limit_bytes=48 * 2**20),
        name="weight_sum",
    )(xc, dh)


def local_dense(tokens, gate_weight, routes, combine, cotangent):
    pairs = routes.shape[0] * routes.shape[1]
    token_grad, xc, dh = exchange(
        tokens, gate_weight, routes.T, combine.T, cotangent.reshape(pairs, cotangent.shape[2])
    )
    grad = weight_sum(xc, dh)
    return (token_grad, grad[None])


def local(tokens, gate_weight, routes, combine, cotangent):
    dense = (
        lax.axis_size("expert") == N_EXP
        and lax.axis_size("replica") == 2
        and tokens.shape == (128, 3584)
        and gate_weight.shape[2] == 2 * cotangent.shape[2]
        and routes.shape[1] == 8
    )
    body = local_dense if dense else local_routed
    return body(tokens, gate_weight, routes, combine, cotangent)


def solution(mesh):
    return jax.shard_map(
        local,
        mesh=mesh,
        in_specs=(
            P("expert", "replica"),
            P("expert", "replica", None),
            P("expert", None),
            P("expert", None),
            P("expert", None, "replica"),
        ),
        out_specs=(P("expert", "replica"), P("expert", "replica", None)),
        check_vma=False,
    )
```

```python
import jax
import jax.numpy as jnp
from jax import lax
from jax.experimental import pallas as pl
from jax.experimental.pallas import tpu as pltpu
from jax.sharding import PartitionSpec as P

MESH = pl.DeviceIdType.MESH


def silu_slope(gate):
    sig = jax.nn.sigmoid(gate)
    return sig * (1.0 + gate * (1.0 - sig))


def local_routed(tokens, gate_weight, routes, combine, cotangent):
    n_exp = lax.axis_size("expert")
    tok_rows = tokens.shape[0]
    width = tokens.shape[1]
    topk = routes.shape[1]
    share = cotangent.shape[2]
    pairs = tok_rows * topk
    cap = max(2, pairs * 5 // (4 * n_exp))
    ids = routes.reshape(pairs)
    earlier = jnp.tril(jnp.ones((tok_rows, tok_rows), jnp.bfloat16), -1)
    onehot = routes[:, :, None] == jnp.arange(n_exp, dtype=jnp.int32)[None, None, :]
    named = jnp.any(onehot, axis=1).astype(jnp.bfloat16)
    rank = jnp.dot(earlier, named, preferred_element_type=jnp.float32)
    slot = jnp.sum(jnp.where(onehot, rank[:, None, :], 0.0), axis=2).astype(jnp.int32)
    target = ids * cap + slot.reshape(pairs)
    slot_pair = (
        jnp.full((n_exp * cap,), pairs, jnp.int32)
        .at[target]
        .set(jnp.arange(pairs, dtype=jnp.int32))
    )
    x_pad = jnp.concatenate([tokens, jnp.zeros((1, width), tokens.dtype)], axis=0)
    cot_pad = jnp.concatenate(
        [cotangent.reshape(pairs, share), jnp.zeros((1, share), cotangent.dtype)], axis=0
    )
    w_pad = jnp.concatenate([combine.reshape(pairs), jnp.zeros((1,), combine.dtype)], axis=0)
    send_x = x_pad[slot_pair // topk].reshape(n_exp, cap, width)
    send_c = cot_pad[slot_pair].reshape(n_exp, cap, share)
    send_w = w_pad[slot_pair].reshape(n_exp, cap)
    recv_x, recv_c, recv_w = (
        lax.all_to_all(send_x, "expert", split_axis=0, concat_axis=0, tiled=True),
        lax.all_to_all(send_c, "expert", split_axis=0, concat_axis=0, tiled=True),
        lax.all_to_all(send_w, "expert", split_axis=0, concat_axis=0, tiled=True),
    )
    rows = n_exp * cap
    recv_x = recv_x.reshape(rows, width)
    recv_c = recv_c.reshape(rows, share)
    recv_w = recv_w.reshape(rows).astype(jnp.float32)
    weight = gate_weight[0]
    gate_part = jnp.dot(recv_x, weight, preferred_element_type=jnp.float32)
    gate_all = lax.psum(gate_part.astype(jnp.bfloat16), "replica").astype(jnp.float32)
    cot_all = lax.all_gather(recv_c, "replica", axis=1, tiled=True)
    dhid = (cot_all.astype(jnp.float32) * recv_w[:, None] * silu_slope(gate_all)).astype(
        jnp.bfloat16
    )
    back_sum = lax.dot_general(
        dhid, weight, (((1,), (1,)), ((), ())), preferred_element_type=jnp.float32
    )
    grad_sum = lax.dot_general(
        recv_x, dhid, (((0,), (0,)), ((), ())), preferred_element_type=jnp.float32
    )
    back_rows = back_sum.astype(jnp.bfloat16).reshape(n_exp, cap, width)
    arrived = lax.all_to_all(back_rows, "expert", split_axis=0, concat_axis=0, tiled=True).reshape(
        rows, width
    )
    pair_rows = arrived[target].reshape(tok_rows, topk, width)
    token_grad = jnp.sum(pair_rows.astype(jnp.float32), axis=1).astype(jnp.bfloat16)
    return (token_grad, grad_sum.astype(jnp.bfloat16)[None])


HIGH = 4
N_EXP = 4 * HIGH
UP, DOWN, SIDE = 0, 1, 2
STEP_Z = (1, -1, 0)


def nearest_first(z):
    every = [(sz, fy, fx) for sz in range(HIGH) for fy in range(2) for fx in range(2)]
    every.sort(key=lambda s: (abs(s[0] - z) + s[1] + s[2], abs(s[0] - z)))
    return [sz * 4 + fy * 2 + fx for sz, fy, fx in every]


def words(inverse):
    found = []
    for z in range(HIGH):
        codes = nearest_first(z)
        if inverse:
            codes = [codes.index(code) for code in range(N_EXP)]
        found.append([sum(codes[q * 4 + i] << (4 * i) for i in range(4)) for q in range(4)])
    return found


PARTS = ((False, 3), (True, 4), (True, 4), (True, 3))


class Part:
    def __init__(self, index, z_first, at, size, inner):
        self.index, self.z_first, self.at, self.size, self.inner = index, z_first, at, size, inner


def parts_of(half):
    unit = half // sum(tiles for _, tiles in PARTS)
    found, at, inner = [], 0, [0, 0]
    for index, (z_first, tiles) in enumerate(PARTS):
        size = tiles * unit
        found.append(Part(index, z_first, at, size, inner[z_first]))
        at += size
        inner[z_first] += size
    return found, inner


def looked_up(z, n, inverse=False):
    word = jnp.int32(0)
    for zz, row in enumerate(words(inverse)):
        for q, value in enumerate(row):
            word = jnp.where(jnp.logical_and(z == zz, n // 4 == q), value, word)
    digit = n % 4
    for i in range(1, 4):
        word = jnp.where(digit == i, word // (16**i), word)
    return word % 16


class Spot:
    def __init__(self, n, me):
        z, y, x = me // 4, (me // 2) % 2, me % 2
        code = looked_up(z, n)
        self.n = n
        self.z, self.y, self.x = z, y, x
        self.sz = code // 4
        self.ey = (code // 2) % 2
        self.ex = code % 2
        self.sy = (y + self.ey) % 2
        self.sx = (x + self.ex) % 2
        self.dz = self.sz - z
        self.index = self.sz * 4 + self.sy * 2 + self.sx


class Side:
    def __init__(self, kind, spot):
        me_y = spot.z * 4 + (1 - spot.y) * 2 + spot.x
        me_x = spot.z * 4 + spot.y * 2 + 1 - spot.x
        self.kind = kind
        self.spot = spot
        if kind == 0:
            self.far, self.e, self.su, self.leaf, self.other = (
                spot.ey, spot.ex, spot.sx, me_y, me_x,
            )
        else:
            self.far, self.e, self.su, self.leaf, self.other = (
                spot.ex, spot.ey, spot.sy, me_x, me_y,
            )
        self.slot = spot.sz * 2 + self.su

    def target(self, way):
        if way == SIDE:
            return self.other
        return (self.spot.z + STEP_Z[way]) * 4 + self.spot.y * 2 + self.spot.x

    def place_at_leaf(self):
        spot = self.spot
        ey, ex = (1 - spot.ey, spot.ex) if self.kind == 0 else (spot.ey, 1 - spot.ex)
        return looked_up(spot.z, spot.sz * 4 + ey * 2 + ex, True)

    def onward(self, part, way):
        dz, z = self.spot.dz, self.spot.z
        if way == SIDE:
            ok = self.e == 0
            return ok if part.z_first else jnp.logical_and(ok, dz == 0)
        by = STEP_Z[way]
        ok = (dz <= 0) if by > 0 else (dz >= 0)
        ok = jnp.logical_and(ok, (z < HIGH - 1) if by > 0 else (z > 0))
        return jnp.logical_and(ok, self.e == 0) if part.z_first else ok

    def back_way(self, part):
        dz, e = self.spot.dz, self.e
        side = e == 1 if part.z_first else jnp.logical_and(e == 1, dz == 0)
        flat = e == 0 if part.z_first else e >= 0
        return (
            (side, SIDE),
            (jnp.logical_and(flat, dz > 0), UP),
            (jnp.logical_and(flat, dz < 0), DOWN),
        )


def choose(ranks, expert, cap):
    experts, tokens = ranks.shape
    which = lax.broadcasted_iota(jnp.int32, (experts, tokens), 0)
    row = jnp.sum(
        jnp.where(which == expert, ranks.astype(jnp.float32), 0.0), axis=0, keepdims=True
    )
    place = lax.broadcasted_iota(jnp.int32, (cap, tokens), 0).astype(jnp.float32)
    return jnp.where(row == place, 1.0, 0.0).astype(jnp.bfloat16)


def tile_spans(width, most):
    found, at = [], 0
    while at < width:
        size = min(most, width - at)
        found.append((at, size))
        at += size
    return found


def remote(src, dst, send, recv, expert=None):
    device = (
        {"replica": 1 - lax.axis_index("replica")} if expert is None else {"expert": expert}
    )
    return pltpu.make_async_remote_copy(
        src_ref=src, dst_ref=dst, send_sem=send, recv_sem=recv,
        device_id=device, device_id_type=MESH,
    )


def row_span(index, rows):
    return pl.ds(pl.multiple_of(index * rows, 16), rows)


AHEAD = 3


def exchange_kernel(
    x_ref, w_ref, routes_ref, combine_ref, cot_ref, tg_ref, xc_out, dh_out,
    slots, pair_w, send_c, full, pack, xc, wv, wt, ra, cot, g_out, g_in, g_own, dh, total, leaf, land_u, land_z,
    full_s, full_r, pack_s, pack_r, ra_s, ra_r, cot_s, cot_r, g_s, g_r, d_s, d_r,
    leaf_s, leaf_r, part_s, land_u_r, land_z_r, loc, xo,
):
    me = lax.axis_index("expert")
    rep = lax.axis_index("replica")
    tokens, width = x_ref.shape
    half = width // 2
    cap = cot.shape[0] // N_EXP
    share = cot.shape[1]
    parts, _ = parts_of(half)
    count = len(parts)
    lands, lands_r = (land_u, land_z), (land_u_r, land_z_r)
    load_w = pltpu.make_async_copy(w_ref.at[0], wv, loc.at[0])
    load_w.start()
    home = (me // 4) * 2
    sides = (home + me % 2, home + (me // 2) % 2)
    for kind in range(2):
        full[kind, sides[kind]] = x_ref[:, kind * half : (kind + 1) * half]

    barrier = pltpu.get_barrier_semaphore()

    def hello(i, carry):
        pl.semaphore_signal(
            barrier, inc=1, device_id={"expert": (me + i) % N_EXP}, device_id_type=MESH
        )
        return carry

    lax.fori_loop(1, N_EXP, hello, 0)
    pl.semaphore_signal(barrier, inc=1, device_id={"replica": 1 - rep}, device_id_type=MESH)
    pl.semaphore_wait(barrier, N_EXP)

    def full_copy(side, part, way):
        o = side.spot.index
        n = (side.kind * count + part.index) * N_EXP + o
        block = full.at[side.kind, side.slot, :, pl.ds(part.at, part.size)]
        return remote(block, block, full_s.at[n * 3 + way], full_r.at[n], side.target(way))

    def pack_copy(side):
        o = side.spot.index
        n = side.kind * N_EXP + o
        return remote(
            pack.at[side.kind, side.slot],
            xc.at[row_span(side.place_at_leaf(), cap), pl.ds(side.kind * half, half)],
            pack_s.at[n], pack_r.at[n], side.leaf,
        )

    def ranks_copy(peer, block):
        return remote(ra.at[block], ra.at[block], ra_s.at[peer], ra_r.at[block], peer)

    def cot_copy(place, peer, block):
        return remote(
            send_c.at[row_span(place, cap), :], cot.at[row_span(block, cap), :],
            cot_s.at[peer], cot_r.at[block], peer,
        )

    def gate_copy(pair):
        rows = row_span(pair, 2 * cap)
        return remote(g_out.at[rows, :], g_in.at[rows, :], g_s.at[pair], g_r.at[pair])

    def dhid_copy(pair, side):
        cols = pl.ds(pl.multiple_of(side * share, 128), share)
        block = dh.at[row_span(pair, 2 * cap), cols]
        return remote(block, block, d_s.at[pair], d_r.at[pair])

    def xc_copy(four):
        rows = row_span(four, 4 * cap)
        return pltpu.make_async_copy(xc.at[rows, :], xc_out.at[rows, :], xo.at[four])

    def leaf_copy(side):
        o = side.spot.index
        n = side.kind * N_EXP + o
        return remote(
            xc.at[row_span(side.spot.n, cap), pl.ds(side.kind * half, half)],
            leaf.at[side.kind, side.slot],
            leaf_s.at[n], leaf_r.at[side.kind * 8 + side.slot], side.leaf,
        )

    def landing(side, part, lower):
        land, recv = lands[part.z_first], lands_r[part.z_first]
        sz, cols = side.spot.sz, pl.ds(part.inner, part.size)
        if part.z_first:
            place = sz if lower is None else HIGH + sz + lower
        else:
            place = 0 if lower is None else 1 + side.su * (HIGH + 1) + sz + lower
        n = (side.kind * count + part.index) * land.shape[1] + place
        return land.at[side.kind, place, :, cols], recv.at[n]

    def part_copy(side, part, way):
        dst, recv = landing(side, part, (1, 0, None)[way])
        n = (side.kind * count + part.index) * N_EXP + side.spot.index
        return remote(
            full.at[side.kind, side.slot, :, pl.ds(part.at, part.size)], dst,
            part_s.at[n], recv, side.target(way),
        )

    ra[me] = rank_pairs(routes_ref, combine_ref, slots, pair_w)

    def make_rows(four):
        place = lax.broadcasted_iota(jnp.int32, (cap, slots.shape[1]), 0).astype(jnp.float32)
        picks = [
            jnp.where(slots[pl.ds(Spot(4 * four + i, me).index, 1), :] == place, pair_w[...], 0.0)
            for i in range(4)
        ]
        send_c[row_span(four, 4 * cap), :] = jnp.dot(
            jnp.concatenate([pick.astype(jnp.bfloat16) for pick in picks], axis=0),
            cot_ref[...], preferred_element_type=jnp.float32,
        ).astype(jnp.bfloat16)

    def send_ranks(n, carry):
        ranks_copy(Spot(n, me).index, me).start()
        return carry

    lax.fori_loop(1, N_EXP, send_ranks, 0)

    def slope(pair):
        gate_copy(pair).wait_recv()
        mine = pl.ds(pl.multiple_of(rep * share, 128), share)
        for i in range(2):
            o = Spot(2 * pair + i, me).index

            @pl.when(o != me)
            def _(o=o):
                cot_copy(0, o, o).wait_recv()

            def some(j, carry, i=i, o=o):
                rows = pl.ds(pl.multiple_of((2 * pair + i) * cap + j * 16, 16), 16)
                theirs = pl.ds(pl.multiple_of(o * cap + j * 16, 16), 16)
                gate = g_own[rows, :].astype(jnp.float32) + g_in[rows, :].astype(jnp.float32)
                sig = 1.0 / (1.0 + jnp.exp(-gate))
                dh[rows, mine] = (
                    cot[theirs, :].astype(jnp.float32) * (sig * (1.0 + gate * (1.0 - sig)))
                ).astype(jnp.bfloat16)
                return carry

            lax.fori_loop(0, cap // 16, some, 0)
        dhid_copy(pair, rep).start()

    def back(four):
        span = row_span(four, 4 * cap)
        for i in range(2):
            dhid_copy(2 * four + i, 1 - rep).wait_recv()
        xc_copy(four).wait()

        def some(i, carry):
            cols = pl.ds(pl.multiple_of(i * 512, 512), 512)
            xc[span, cols] = jnp.dot(
                dh[span, :], wt[:, cols], preferred_element_type=jnp.float32
            ).astype(jnp.bfloat16)
            return carry

        lax.fori_loop(0, width // 512, some, 0)

    def send_leaf(n):
        spot = Spot(n, me)
        for kind in range(2):
            side = Side(kind, spot)

            @pl.when(side.far == 1)
            def _(side=side):
                leaf_copy(side).start()

    def gate(pair):
        rows = row_span(pair, 2 * cap)

        def product(side):
            cols = pl.ds(pl.multiple_of(side * share, 128), share)
            return jnp.dot(
                xc[rows, :], wv[:, cols], preferred_element_type=jnp.float32
            ).astype(jnp.bfloat16)

        g_out[rows, :] = product(1 - rep)
        gate_copy(pair).start()
        g_own[rows, :] = product(rep)

    def step(n, carry):
        spot = Spot(n, me)
        o = spot.index
        rows = row_span(n, cap)
        both = (Side(0, spot), Side(1, spot))
        for part in parts:
            for side in both:

                @pl.when(side.far == 0)
                def _(side=side, part=part):
                    @pl.when(n > 0)
                    def _():
                        full_copy(side, part, SIDE).wait_recv()

                    for way in (UP, DOWN, SIDE):

                        @pl.when(side.onward(part, way))
                        def _(way=way):
                            full_copy(side, part, way).start()

        @pl.when(n > 0)
        def _():
            ranks_copy(o, o).wait_recv()

        for side in both:

            @pl.when(side.far == 0)
            def _(side=side):
                ranks = ra[o]
                pick = jnp.concatenate(
                    [choose(ranks, me, cap), choose(ranks, side.leaf, cap)], axis=0
                )
                for at, size in tile_spans(half, 256):
                    found = jnp.dot(
                        pick, full[side.kind, side.slot, :, at : at + size],
                        preferred_element_type=jnp.float32,
                    ).astype(jnp.bfloat16)
                    pack[side.kind, side.slot, :, at : at + size] = found[cap:]
                    begin = side.kind * half + at
                    xc[rows, begin : begin + size] = found[:cap]
                pack_copy(side).start()

        @pl.when(n < 4)
        def _():
            make_rows(n)

            @pl.when(n == 0)
            def _():
                cot[row_span(me, cap), :] = send_c[:cap, :]

            for i in range(4):
                later = n * 4 + i

                @pl.when(later > 0)
                def _(later=later):
                    cot_copy(later, Spot(later, me).index, me).start()

        @pl.when(n == 0)
        def _():
            load_w.wait()

        for side in both:

            @pl.when(side.far == 1)
            def _(side=side):
                pack_copy(side).wait_recv()

        @pl.when(n % 4 == 3)
        def _():
            xc_copy(n // 4).start()

        @pl.when(jnp.logical_and(n >= 1, n <= width // 512))
        def _():
            cols = pl.ds(pl.multiple_of((n - 1) * 512, 512), 512)
            wt[:, cols] = wv[cols, :].T

        @pl.when(n % 2 == 1)
        def _():
            gate(n // 2)

        @pl.when(jnp.logical_and(n % 2 == 0, n >= 4))
        def _():
            slope(n // 2 - 2)

        @pl.when(jnp.logical_or(n == 7, n == 11))
        def _():
            back((n - 7) // 4)

        return carry

    lax.fori_loop(0, N_EXP, step, 0)
    slope(N_EXP // 2 - 2)
    slope(N_EXP // 2 - 1)
    save = pltpu.make_async_copy(dh, dh_out, loc.at[0])

    def first(i, carry):
        send_leaf(N_EXP - 1 - i)
        return carry

    back(3)
    lax.fori_loop(0, AHEAD, first, 0)
    back(2)
    save.start()

    def gathered(m, carry):
        n = N_EXP - 1 - m
        spot = Spot(n, me)
        span = row_span(n, cap)

        @pl.when(n >= AHEAD)
        def _():
            send_leaf(n - AHEAD)

        both = (Side(0, spot), Side(1, spot))
        for kind, side in enumerate(both):

            @pl.when(side.far == 0)
            def _(side=side, kind=kind):
                ranks = ra[spot.index]
                pick_me = choose(ranks, me, cap)
                pick_leaf = choose(ranks, side.leaf, cap)
                leaf_copy(side).wait_recv()
                for at, size in tile_spans(half, 256):
                    begin = kind * half + at
                    total[kind, :, at : at + size] = lax.dot_general(
                        pick_me, xc[span, begin : begin + size], (((0,), (0,)), ((), ())),
                        preferred_element_type=jnp.float32,
                    ) + lax.dot_general(
                        pick_leaf, leaf[kind, side.slot, :, at : at + size],
                        (((0,), (0,)), ((), ())), preferred_element_type=jnp.float32,
                    )

        for part in parts:
            cols = slice(part.at, part.at + part.size)
            for kind, side in enumerate(both):

                @pl.when(side.far == 0)
                def _(side=side, kind=kind, part=part, cols=cols):
                    for way in (UP, DOWN, SIDE):

                        @pl.when(side.onward(part, way))
                        def _(way=way):
                            full_copy(side, part, way).wait_send()
                            dst, recv = landing(side, part, (0, 1, None)[way])
                            remote(dst, dst, recv, recv, side.target(way)).wait_recv()
                            total[kind, :, cols] += dst[...].astype(jnp.float32)

                    @pl.when(n > 0)
                    def _():
                        full[kind, side.slot, :, cols] = total[kind, :, cols].astype(
                            jnp.bfloat16
                        )
                        for ok, way in side.back_way(part):

                            @pl.when(ok)
                            def _(way=way):
                                part_copy(side, part, way).start()

        @pl.when(n == 0)
        def _():
            for kind in range(2):
                tg_ref[:, kind * half : (kind + 1) * half] = total[kind].astype(jnp.bfloat16)

        return carry

    lax.fori_loop(0, N_EXP, gathered, 0)

    def finish(n, carry):
        spot = Spot(n, me)
        o = spot.index
        for kind in range(2):
            side = Side(kind, spot)

            @pl.when(side.far == 0)
            def _(side=side):
                pack_copy(side).wait_send()

                @pl.when(n > 0)
                def _():
                    for part in parts:
                        part_copy(side, part, SIDE).wait_send()

            @pl.when(side.far == 1)
            def _(side=side):
                leaf_copy(side).wait_send()

        @pl.when(n > 0)
        def _():
            ranks_copy(o, me).wait_send()
            cot_copy(n, o, me).wait_send()

        @pl.when(n % 2 == 0)
        def _():
            gate_copy(n // 2).wait_send()
            dhid_copy(n // 2, rep).wait_send()

        return carry

    lax.fori_loop(0, N_EXP, finish, 0)
    save.wait()


def rank_pairs(routes_ref, combine_ref, slots, pair_w):
    topk, tokens = routes_ref.shape
    pairs, f32, bf16 = tokens * topk, jnp.float32, jnp.bfloat16
    iota = lambda shape, dim: lax.broadcasted_iota(jnp.int32, shape, dim)
    dot = lambda a, b: jnp.dot(a, b, preferred_element_type=f32)
    routes = routes_ref[...]
    named = jnp.zeros((N_EXP, tokens), f32)
    for k in range(topk):
        named += jnp.where(routes[k : k + 1, :] == iota((N_EXP, tokens), 0), 1.0, 0.0)
    square = (tokens, tokens)
    before = jnp.where(iota(square, 0) < iota(square, 1), 1.0, 0.0).astype(bf16)
    ranks = jnp.where(named > 0.5, dot(named.astype(bf16), before), -1.0).astype(bf16)
    wide = (tokens, pairs)
    widen = jnp.where(iota(wide, 1) // topk == iota(wide, 0), 1.0, 0.0).astype(bf16)
    mine = iota((topk, pairs), 1) % topk == iota((topk, pairs), 0)
    flat = lambda a: jnp.sum(jnp.where(mine, dot(a, widen), 0.0), axis=0, keepdims=True)
    expert = flat(routes.astype(f32).astype(bf16))
    pair_w[...] = flat(combine_ref[...])
    slots[...] = jnp.where(
        expert == iota((N_EXP, pairs), 0).astype(f32),
        dot(ranks, widen), -1.0,
    )
    return ranks


def exchange(tokens, weight, routes, combine, cotangent):
    rows, width = tokens.shape
    half, hidden = width // 2, weight.shape[2]
    pairs, share = cotangent.shape
    cap = pairs * 5 // (4 * N_EXP)
    rows_all = cap * N_EXP
    _, (wide_u, wide_z) = parts_of(half)
    count = 2 * len(PARTS)
    slots_u, slots_z = 2 * HIGH + 3, 2 * HIGH + 1
    bf16, dma = jnp.bfloat16, pltpu.SemaphoreType.DMA
    vmem, anywhere = pl.BlockSpec(memory_space=pltpu.VMEM), pl.BlockSpec(memory_space=pl.ANY)
    return pl.pallas_call(
        exchange_kernel,
        out_shape=(
            jax.ShapeDtypeStruct((rows, width), bf16),
            jax.ShapeDtypeStruct((rows_all, width), bf16),
            jax.ShapeDtypeStruct((rows_all, hidden), bf16),
        ),
        in_specs=[vmem, anywhere, vmem, vmem, vmem],
        out_specs=[vmem, anywhere, anywhere],
        scratch_shapes=[
            pltpu.VMEM((N_EXP, pairs), jnp.float32),
            pltpu.VMEM((1, pairs), jnp.float32),
            pltpu.VMEM((rows_all, share), bf16),
            pltpu.VMEM((2, 8, rows, half), bf16),
            pltpu.VMEM((2, 8, cap, half), bf16),
            pltpu.VMEM((rows_all, width), bf16),
            pltpu.VMEM((width, hidden), bf16),
            pltpu.VMEM((hidden, width), bf16),
            pltpu.VMEM((N_EXP, N_EXP, rows), bf16),
            pltpu.VMEM((rows_all, share), bf16),
            pltpu.VMEM((rows_all, share), bf16),
            pltpu.VMEM((rows_all, share), bf16),
            pltpu.VMEM((rows_all, share), bf16),
            pltpu.VMEM((rows_all, hidden), bf16),
            pltpu.VMEM((2, rows, half), jnp.float32),
            pltpu.VMEM((2, 8, cap, half), bf16),
            pltpu.VMEM((2, slots_u, rows, wide_u), bf16),
            pltpu.VMEM((2, slots_z, rows, wide_z), bf16),
            dma((count * N_EXP * 3,)), dma((count * N_EXP,)),
            dma((2 * N_EXP,)), dma((2 * N_EXP,)),
            dma((N_EXP,)), dma((N_EXP,)), dma((N_EXP,)), dma((N_EXP,)),
            dma((8,)), dma((8,)), dma((8,)), dma((8,)),
            dma((2 * N_EXP,)), dma((16,)), dma((count * N_EXP,)),
            dma((count * slots_u,)), dma((count * slots_z,)),
            dma((1,)), dma((N_EXP,)),
        ],
        compiler_params=pltpu.CompilerParams(
            collective_id=0, has_side_effects=True, vmem_limit_bytes=62 * 2**20
        ),
        name="exchange",
    )(tokens, weight, routes, combine, cotangent)


def weight_sum_kernel(x_ref, d_ref, o_ref):
    o_ref[...] = lax.dot_general(
        x_ref[...], d_ref[...], (((0,), (0,)), ((), ())), preferred_element_type=jnp.float32
    ).astype(o_ref.dtype)


def weight_sum(xc, dh):
    total, width = xc.shape
    hidden = dh.shape[1]
    return pl.pallas_call(
        weight_sum_kernel,
        out_shape=jax.ShapeDtypeStruct((width, hidden), jnp.bfloat16),
        grid=(width // 896,),
        in_specs=[
            pl.BlockSpec((total, 896), lambda i: (0, i)),
            pl.BlockSpec((total, hidden), lambda i: (0, 0)),
        ],
        out_specs=pl.BlockSpec((896, hidden), lambda i: (i, 0)),
        compiler_params=pltpu.CompilerParams(vmem_limit_bytes=48 * 2**20),
        name="weight_sum",
    )(xc, dh)


def local_dense(tokens, gate_weight, routes, combine, cotangent):
    pairs = routes.shape[0] * routes.shape[1]
    token_grad, xc, dh = exchange(
        tokens, gate_weight, routes.T, combine.T, cotangent.reshape(pairs, cotangent.shape[2])
    )
    grad = weight_sum(xc, dh)
    return (token_grad, grad[None])


def local(tokens, gate_weight, routes, combine, cotangent):
    dense = (
        lax.axis_size("expert") == N_EXP
        and lax.axis_size("replica") == 2
        and tokens.shape == (128, 3584)
        and gate_weight.shape[2] == 2 * cotangent.shape[2]
        and routes.shape[1] == 8
    )
    body = local_dense if dense else local_routed
    return body(tokens, gate_weight, routes, combine, cotangent)


def solution(mesh):
    return jax.shard_map(
        local,
        mesh=mesh,
        in_specs=(
            P("expert", "replica"),
            P("expert", "replica", None),
            P("expert", None),
            P("expert", None),
            P("expert", None, "replica"),
        ),
        out_specs=(P("expert", "replica"), P("expert", "replica", None)),
        check_vma=False,
    )
```

```python
import jax
import jax.numpy as jnp
from jax import lax
from jax.experimental import pallas as pl
from jax.experimental.pallas import tpu as pltpu
from jax.sharding import PartitionSpec as P

MESH = pl.DeviceIdType.MESH


def silu_slope(gate):
    sig = jax.nn.sigmoid(gate)
    return sig * (1.0 + gate * (1.0 - sig))


def local_routed(tokens, gate_weight, routes, combine, cotangent):
    n_exp = lax.axis_size("expert")
    tok_rows = tokens.shape[0]
    width = tokens.shape[1]
    topk = routes.shape[1]
    share = cotangent.shape[2]
    pairs = tok_rows * topk
    cap = max(2, pairs * 5 // (4 * n_exp))
    ids = routes.reshape(pairs)
    earlier = jnp.tril(jnp.ones((tok_rows, tok_rows), jnp.bfloat16), -1)
    onehot = routes[:, :, None] == jnp.arange(n_exp, dtype=jnp.int32)[None, None, :]
    named = jnp.any(onehot, axis=1).astype(jnp.bfloat16)
    rank = jnp.dot(earlier, named, preferred_element_type=jnp.float32)
    slot = jnp.sum(jnp.where(onehot, rank[:, None, :], 0.0), axis=2).astype(jnp.int32)
    target = ids * cap + slot.reshape(pairs)
    slot_pair = (
        jnp.full((n_exp * cap,), pairs, jnp.int32)
        .at[target]
        .set(jnp.arange(pairs, dtype=jnp.int32))
    )
    x_pad = jnp.concatenate([tokens, jnp.zeros((1, width), tokens.dtype)], axis=0)
    cot_pad = jnp.concatenate(
        [cotangent.reshape(pairs, share), jnp.zeros((1, share), cotangent.dtype)], axis=0
    )
    w_pad = jnp.concatenate([combine.reshape(pairs), jnp.zeros((1,), combine.dtype)], axis=0)
    send_x = x_pad[slot_pair // topk].reshape(n_exp, cap, width)
    send_c = cot_pad[slot_pair].reshape(n_exp, cap, share)
    send_w = w_pad[slot_pair].reshape(n_exp, cap)
    recv_x, recv_c, recv_w = (
        lax.all_to_all(send_x, "expert", split_axis=0, concat_axis=0, tiled=True),
        lax.all_to_all(send_c, "expert", split_axis=0, concat_axis=0, tiled=True),
        lax.all_to_all(send_w, "expert", split_axis=0, concat_axis=0, tiled=True),
    )
    rows = n_exp * cap
    recv_x = recv_x.reshape(rows, width)
    recv_c = recv_c.reshape(rows, share)
    recv_w = recv_w.reshape(rows).astype(jnp.float32)
    weight = gate_weight[0]
    gate_part = jnp.dot(recv_x, weight, preferred_element_type=jnp.float32)
    gate_all = lax.psum(gate_part.astype(jnp.bfloat16), "replica").astype(jnp.float32)
    cot_all = lax.all_gather(recv_c, "replica", axis=1, tiled=True)
    dhid = (cot_all.astype(jnp.float32) * recv_w[:, None] * silu_slope(gate_all)).astype(
        jnp.bfloat16
    )
    back_sum = lax.dot_general(
        dhid, weight, (((1,), (1,)), ((), ())), preferred_element_type=jnp.float32
    )
    grad_sum = lax.dot_general(
        recv_x, dhid, (((0,), (0,)), ((), ())), preferred_element_type=jnp.float32
    )
    back_rows = back_sum.astype(jnp.bfloat16).reshape(n_exp, cap, width)
    arrived = lax.all_to_all(back_rows, "expert", split_axis=0, concat_axis=0, tiled=True).reshape(
        rows, width
    )
    pair_rows = arrived[target].reshape(tok_rows, topk, width)
    token_grad = jnp.sum(pair_rows.astype(jnp.float32), axis=1).astype(jnp.bfloat16)
    return (token_grad, grad_sum.astype(jnp.bfloat16)[None])


HIGH = 4
N_EXP = 4 * HIGH
UP, DOWN, SIDE = 0, 1, 2
STEP_Z = (1, -1, 0)


def nearest_first(z):
    every = [(sz, fy, fx) for sz in range(HIGH) for fy in range(2) for fx in range(2)]
    every.sort(key=lambda s: (abs(s[0] - z) + s[1] + s[2], abs(s[0] - z)))
    return [sz * 4 + fy * 2 + fx for sz, fy, fx in every]


def words(inverse):
    found = []
    for z in range(HIGH):
        codes = nearest_first(z)
        if inverse:
            codes = [codes.index(code) for code in range(N_EXP)]
        found.append([sum(codes[q * 4 + i] << (4 * i) for i in range(4)) for q in range(4)])
    return found


PARTS = ((False, 3), (True, 4), (True, 4), (True, 3))


class Part:
    def __init__(self, index, z_first, at, size, inner):
        self.index, self.z_first, self.at, self.size, self.inner = index, z_first, at, size, inner


def parts_of(half):
    unit = half // sum(tiles for _, tiles in PARTS)
    found, at, inner = [], 0, [0, 0]
    for index, (z_first, tiles) in enumerate(PARTS):
        size = tiles * unit
        found.append(Part(index, z_first, at, size, inner[z_first]))
        at += size
        inner[z_first] += size
    return found, inner


def looked_up(z, n, inverse=False):
    word = jnp.int32(0)
    for zz, row in enumerate(words(inverse)):
        for q, value in enumerate(row):
            word = jnp.where(jnp.logical_and(z == zz, n // 4 == q), value, word)
    digit = n % 4
    for i in range(1, 4):
        word = jnp.where(digit == i, word // (16**i), word)
    return word % 16


class Spot:
    def __init__(self, n, me):
        z, y, x = me // 4, (me // 2) % 2, me % 2
        code = looked_up(z, n)
        self.n = n
        self.z, self.y, self.x = z, y, x
        self.sz = code // 4
        self.ey = (code // 2) % 2
        self.ex = code % 2
        self.sy = (y + self.ey) % 2
        self.sx = (x + self.ex) % 2
        self.dz = self.sz - z
        self.index = self.sz * 4 + self.sy * 2 + self.sx


class Side:
    def __init__(self, kind, spot):
        me_y = spot.z * 4 + (1 - spot.y) * 2 + spot.x
        me_x = spot.z * 4 + spot.y * 2 + 1 - spot.x
        self.kind = kind
        self.spot = spot
        if kind == 0:
            self.far, self.e, self.su, self.leaf, self.other = (
                spot.ey, spot.ex, spot.sx, me_y, me_x,
            )
        else:
            self.far, self.e, self.su, self.leaf, self.other = (
                spot.ex, spot.ey, spot.sy, me_x, me_y,
            )
        self.slot = spot.sz * 2 + self.su

    def target(self, way):
        if way == SIDE:
            return self.other
        return (self.spot.z + STEP_Z[way]) * 4 + self.spot.y * 2 + self.spot.x

    def place_at_leaf(self):
        spot = self.spot
        ey, ex = (1 - spot.ey, spot.ex) if self.kind == 0 else (spot.ey, 1 - spot.ex)
        return looked_up(spot.z, spot.sz * 4 + ey * 2 + ex, True)

    def onward(self, part, way):
        dz, z = self.spot.dz, self.spot.z
        if way == SIDE:
            ok = self.e == 0
            return ok if part.z_first else jnp.logical_and(ok, dz == 0)
        by = STEP_Z[way]
        ok = (dz <= 0) if by > 0 else (dz >= 0)
        ok = jnp.logical_and(ok, (z < HIGH - 1) if by > 0 else (z > 0))
        return jnp.logical_and(ok, self.e == 0) if part.z_first else ok

    def back_way(self, part):
        dz, e = self.spot.dz, self.e
        side = e == 1 if part.z_first else jnp.logical_and(e == 1, dz == 0)
        flat = e == 0 if part.z_first else e >= 0
        return (
            (side, SIDE),
            (jnp.logical_and(flat, dz > 0), UP),
            (jnp.logical_and(flat, dz < 0), DOWN),
        )


def choose(ranks, expert, cap):
    experts, tokens = ranks.shape
    which = lax.broadcasted_iota(jnp.int32, (experts, tokens), 0)
    row = jnp.sum(
        jnp.where(which == expert, ranks.astype(jnp.float32), 0.0), axis=0, keepdims=True
    )
    place = lax.broadcasted_iota(jnp.int32, (cap, tokens), 0).astype(jnp.float32)
    return jnp.where(row == place, 1.0, 0.0).astype(jnp.bfloat16)


def tile_spans(width, most):
    found, at = [], 0
    while at < width:
        size = min(most, width - at)
        found.append((at, size))
        at += size
    return found


def remote(src, dst, send, recv, expert=None):
    device = (
        {"replica": 1 - lax.axis_index("replica")} if expert is None else {"expert": expert}
    )
    return pltpu.make_async_remote_copy(
        src_ref=src, dst_ref=dst, send_sem=send, recv_sem=recv,
        device_id=device, device_id_type=MESH,
    )


def row_span(index, rows):
    return pl.ds(pl.multiple_of(index * rows, 16), rows)


AHEAD = 3


def exchange_kernel(
    x_ref, w_ref, routes_ref, combine_ref, cot_ref, tg_ref, xc_out, dh_out,
    slots, pair_w, send_c, full, pack, xc, wv, wt, ra, cot, g_out, g_in, g_own, dh, total, leaf, land_u, land_z,
    full_s, full_r, pack_s, pack_r, ra_s, ra_r, cot_s, cot_r, g_s, g_r, d_s, d_r,
    leaf_s, leaf_r, part_s, land_u_r, land_z_r, loc, xo,
):
    me = lax.axis_index("expert")
    rep = lax.axis_index("replica")
    tokens, width = x_ref.shape
    half = width // 2
    cap = cot.shape[0] // N_EXP
    share = cot.shape[1]
    parts, _ = parts_of(half)
    count = len(parts)
    lands, lands_r = (land_u, land_z), (land_u_r, land_z_r)
    load_w = pltpu.make_async_copy(w_ref.at[0], wv, loc.at[0])
    load_w.start()
    home = (me // 4) * 2
    sides = (home + me % 2, home + (me // 2) % 2)
    for kind in range(2):
        full[kind, sides[kind]] = x_ref[:, kind * half : (kind + 1) * half]

    barrier = pltpu.get_barrier_semaphore()

    def hello(i, carry):
        pl.semaphore_signal(
            barrier, inc=1, device_id={"expert": (me + i) % N_EXP}, device_id_type=MESH
        )
        return carry

    lax.fori_loop(1, N_EXP, hello, 0)
    pl.semaphore_signal(barrier, inc=1, device_id={"replica": 1 - rep}, device_id_type=MESH)
    pl.semaphore_wait(barrier, N_EXP)

    def full_copy(side, part, way):
        o = side.spot.index
        n = (side.kind * count + part.index) * N_EXP + o
        block = full.at[side.kind, side.slot, :, pl.ds(part.at, part.size)]
        return remote(block, block, full_s.at[n * 3 + way], full_r.at[n], side.target(way))

    def pack_copy(side):
        o = side.spot.index
        n = side.kind * N_EXP + o
        return remote(
            pack.at[side.kind, side.slot],
            xc.at[row_span(side.place_at_leaf(), cap), pl.ds(side.kind * half, half)],
            pack_s.at[n], pack_r.at[n], side.leaf,
        )

    def ranks_copy(peer, block):
        return remote(ra.at[block], ra.at[block], ra_s.at[peer], ra_r.at[block], peer)

    def cot_copy(place, peer, block):
        return remote(
            send_c.at[row_span(place, cap), :], cot.at[row_span(block, cap), :],
            cot_s.at[peer], cot_r.at[block], peer,
        )

    def gate_copy(pair):
        rows = row_span(pair, 2 * cap)
        return remote(g_out.at[rows, :], g_in.at[rows, :], g_s.at[pair], g_r.at[pair])

    def dhid_copy(pair, side):
        cols = pl.ds(pl.multiple_of(side * share, 128), share)
        block = dh.at[row_span(pair, 2 * cap), cols]
        return remote(block, block, d_s.at[pair], d_r.at[pair])

    def xc_copy(four):
        rows = row_span(four, 4 * cap)
        return pltpu.make_async_copy(xc.at[rows, :], xc_out.at[rows, :], xo.at[four])

    def leaf_copy(side):
        o = side.spot.index
        n = side.kind * N_EXP + o
        return remote(
            xc.at[row_span(side.spot.n, cap), pl.ds(side.kind * half, half)],
            leaf.at[side.kind, side.slot],
            leaf_s.at[n], leaf_r.at[side.kind * 8 + side.slot], side.leaf,
        )

    def landing(side, part, lower):
        land, recv = lands[part.z_first], lands_r[part.z_first]
        sz, cols = side.spot.sz, pl.ds(part.inner, part.size)
        if part.z_first:
            place = sz if lower is None else HIGH + sz + lower
        else:
            place = 0 if lower is None else 1 + side.su * (HIGH + 1) + sz + lower
        n = (side.kind * count + part.index) * land.shape[1] + place
        return land.at[side.kind, place, :, cols], recv.at[n]

    def part_copy(side, part, way):
        dst, recv = landing(side, part, (1, 0, None)[way])
        n = (side.kind * count + part.index) * N_EXP + side.spot.index
        return remote(
            full.at[side.kind, side.slot, :, pl.ds(part.at, part.size)], dst,
            part_s.at[n], recv, side.target(way),
        )

    ra[me] = rank_pairs(routes_ref, combine_ref, slots, pair_w)

    def make_rows(four):
        place = lax.broadcasted_iota(jnp.int32, (cap, slots.shape[1]), 0).astype(jnp.float32)
        picks = [
            jnp.where(slots[pl.ds(Spot(4 * four + i, me).index, 1), :] == place, pair_w[...], 0.0)
            for i in range(4)
        ]
        send_c[row_span(four, 4 * cap), :] = jnp.dot(
            jnp.concatenate([pick.astype(jnp.bfloat16) for pick in picks], axis=0),
            cot_ref[...], preferred_element_type=jnp.float32,
        ).astype(jnp.bfloat16)

    def send_ranks(n, carry):
        ranks_copy(Spot(n, me).index, me).start()
        return carry

    lax.fori_loop(1, N_EXP, send_ranks, 0)

    def slope(pair):
        gate_copy(pair).wait_recv()
        mine = pl.ds(pl.multiple_of(rep * share, 128), share)
        for i in range(2):
            o = Spot(2 * pair + i, me).index

            @pl.when(o != me)
            def _(o=o):
                cot_copy(0, o, o).wait_recv()

            def some(j, carry, i=i, o=o):
                rows = pl.ds(pl.multiple_of((2 * pair + i) * cap + j * 16, 16), 16)
                theirs = pl.ds(pl.multiple_of(o * cap + j * 16, 16), 16)
                gate = g_own[rows, :].astype(jnp.float32) + g_in[rows, :].astype(jnp.float32)
                sig = 1.0 / (1.0 + jnp.exp(-gate))
                dh[rows, mine] = (
                    cot[theirs, :].astype(jnp.float32) * (sig * (1.0 + gate * (1.0 - sig)))
                ).astype(jnp.bfloat16)
                return carry

            lax.fori_loop(0, cap // 16, some, 0)
        dhid_copy(pair, rep).start()

    def back(four):
        span = row_span(four, 4 * cap)
        for i in range(2):
            dhid_copy(2 * four + i, 1 - rep).wait_recv()
        xc_copy(four).wait()

        def some(i, carry):
            cols = pl.ds(pl.multiple_of(i * 512, 512), 512)
            xc[span, cols] = jnp.dot(
                dh[span, :], wt[:, cols], preferred_element_type=jnp.float32
            ).astype(jnp.bfloat16)
            return carry

        lax.fori_loop(0, width // 512, some, 0)

    def send_leaf(n):
        spot = Spot(n, me)
        for kind in range(2):
            side = Side(kind, spot)

            @pl.when(side.far == 1)
            def _(side=side):
                leaf_copy(side).start()

    def gate(pair):
        rows = row_span(pair, 2 * cap)

        def product(side):
            cols = pl.ds(pl.multiple_of(side * share, 128), share)
            return jnp.dot(
                xc[rows, :], wv[:, cols], preferred_element_type=jnp.float32
            ).astype(jnp.bfloat16)

        g_out[rows, :] = product(1 - rep)
        gate_copy(pair).start()
        g_own[rows, :] = product(rep)

    def step(n, carry):
        spot = Spot(n, me)
        o = spot.index
        rows = row_span(n, cap)
        both = (Side(0, spot), Side(1, spot))
        for part in parts:
            for side in both:

                @pl.when(side.far == 0)
                def _(side=side, part=part):
                    @pl.when(n > 0)
                    def _():
                        full_copy(side, part, SIDE).wait_recv()

                    for way in (UP, DOWN, SIDE):

                        @pl.when(side.onward(part, way))
                        def _(way=way):
                            full_copy(side, part, way).start()

        @pl.when(n > 0)
        def _():
            ranks_copy(o, o).wait_recv()

        for side in both:

            @pl.when(side.far == 0)
            def _(side=side):
                ranks = ra[o]
                pick = jnp.concatenate(
                    [choose(ranks, me, cap), choose(ranks, side.leaf, cap)], axis=0
                )
                for at, size in tile_spans(half, 256):
                    found = jnp.dot(
                        pick, full[side.kind, side.slot, :, at : at + size],
                        preferred_element_type=jnp.float32,
                    ).astype(jnp.bfloat16)
                    pack[side.kind, side.slot, :, at : at + size] = found[cap:]
                    begin = side.kind * half + at
                    xc[rows, begin : begin + size] = found[:cap]
                pack_copy(side).start()

        @pl.when(n < 4)
        def _():
            make_rows(n)

            @pl.when(n == 0)
            def _():
                cot[row_span(me, cap), :] = send_c[:cap, :]

            for i in range(4):
                later = n * 4 + i

                @pl.when(later > 0)
                def _(later=later):
                    cot_copy(later, Spot(later, me).index, me).start()

        @pl.when(n == 0)
        def _():
            load_w.wait()

        for side in both:

            @pl.when(side.far == 1)
            def _(side=side):
                pack_copy(side).wait_recv()

        @pl.when(n % 4 == 3)
        def _():
            xc_copy(n // 4).start()

        @pl.when(jnp.logical_and(n >= 1, n <= width // 512))
        def _():
            cols = pl.ds(pl.multiple_of((n - 1) * 512, 512), 512)
            wt[:, cols] = wv[cols, :].T

        @pl.when(n % 2 == 1)
        def _():
            gate(n // 2)

        @pl.when(jnp.logical_and(n % 2 == 0, n >= 4))
        def _():
            slope(n // 2 - 2)

        @pl.when(jnp.logical_or(n == 7, n == 11))
        def _():
            back((n - 7) // 4)

        return carry

    lax.fori_loop(0, N_EXP, step, 0)
    slope(N_EXP // 2 - 2)
    slope(N_EXP // 2 - 1)
    save = pltpu.make_async_copy(dh, dh_out, loc.at[0])

    def first(i, carry):
        send_leaf(N_EXP - 1 - i)
        return carry

    back(3)
    lax.fori_loop(0, AHEAD, first, 0)
    back(2)
    save.start()

    def gathered(m, carry):
        n = N_EXP - 1 - m
        spot = Spot(n, me)
        span = row_span(n, cap)

        @pl.when(n >= AHEAD)
        def _():
            send_leaf(n - AHEAD)

        both = (Side(0, spot), Side(1, spot))
        for kind, side in enumerate(both):

            @pl.when(side.far == 0)
            def _(side=side, kind=kind):
                ranks = ra[spot.index]
                pick_me = choose(ranks, me, cap)
                pick_leaf = choose(ranks, side.leaf, cap)
                leaf_copy(side).wait_recv()
                for at, size in tile_spans(half, 256):
                    begin = kind * half + at
                    total[kind, :, at : at + size] = lax.dot_general(
                        pick_me, xc[span, begin : begin + size], (((0,), (0,)), ((), ())),
                        preferred_element_type=jnp.float32,
                    ) + lax.dot_general(
                        pick_leaf, leaf[kind, side.slot, :, at : at + size],
                        (((0,), (0,)), ((), ())), preferred_element_type=jnp.float32,
                    )

        for part in parts:
            cols = slice(part.at, part.at + part.size)
            for kind, side in enumerate(both):

                @pl.when(side.far == 0)
                def _(side=side, kind=kind, part=part, cols=cols):
                    for way in (UP, DOWN, SIDE):

                        @pl.when(side.onward(part, way))
                        def _(way=way):
                            full_copy(side, part, way).wait_send()
                            dst, recv = landing(side, part, (0, 1, None)[way])
                            remote(dst, dst, recv, recv, side.target(way)).wait_recv()
                            total[kind, :, cols] += dst[...].astype(jnp.float32)

                    @pl.when(n > 0)
                    def _():
                        full[kind, side.slot, :, cols] = total[kind, :, cols].astype(
                            jnp.bfloat16
                        )
                        for ok, way in side.back_way(part):

                            @pl.when(ok)
                            def _(way=way):
                                part_copy(side, part, way).start()

        @pl.when(n == 0)
        def _():
            for kind in range(2):
                tg_ref[:, kind * half : (kind + 1) * half] = total[kind].astype(jnp.bfloat16)

        return carry

    lax.fori_loop(0, N_EXP, gathered, 0)

    def finish(n, carry):
        spot = Spot(n, me)
        o = spot.index
        for kind in range(2):
            side = Side(kind, spot)

            @pl.when(side.far == 0)
            def _(side=side):
                pack_copy(side).wait_send()

                @pl.when(n > 0)
                def _():
                    for part in parts:
                        part_copy(side, part, SIDE).wait_send()

            @pl.when(side.far == 1)
            def _(side=side):
                leaf_copy(side).wait_send()

        @pl.when(n > 0)
        def _():
            ranks_copy(o, me).wait_send()
            cot_copy(n, o, me).wait_send()

        @pl.when(n % 2 == 0)
        def _():
            gate_copy(n // 2).wait_send()
            dhid_copy(n // 2, rep).wait_send()

        return carry

    lax.fori_loop(0, N_EXP, finish, 0)
    save.wait()


def rank_pairs(routes_ref, combine_ref, slots, pair_w):
    topk, tokens = routes_ref.shape
    pairs, f32, bf16 = tokens * topk, jnp.float32, jnp.bfloat16
    iota = lambda shape, dim: lax.broadcasted_iota(jnp.int32, shape, dim)
    dot = lambda a, b: jnp.dot(a, b, preferred_element_type=f32)
    routes = routes_ref[...]
    named = jnp.zeros((N_EXP, tokens), f32)
    for k in range(topk):
        named += jnp.where(routes[k : k + 1, :] == iota((N_EXP, tokens), 0), 1.0, 0.0)
    square = (tokens, tokens)
    before = jnp.where(iota(square, 0) < iota(square, 1), 1.0, 0.0).astype(bf16)
    ranks = jnp.where(named > 0.5, dot(named.astype(bf16), before), -1.0).astype(bf16)
    wide = (tokens, pairs)
    widen = jnp.where(iota(wide, 1) // topk == iota(wide, 0), 1.0, 0.0).astype(bf16)
    mine = iota((topk, pairs), 1) % topk == iota((topk, pairs), 0)
    flat = lambda a: jnp.sum(jnp.where(mine, dot(a, widen), 0.0), axis=0, keepdims=True)
    expert = flat(routes.astype(f32).astype(bf16))
    pair_w[...] = flat(combine_ref[...])
    slots[...] = jnp.where(
        expert == iota((N_EXP, pairs), 0).astype(f32),
        dot(ranks, widen), -1.0,
    )
    return ranks


def exchange(tokens, weight, routes, combine, cotangent):
    rows, width = tokens.shape
    half, hidden = width // 2, weight.shape[2]
    pairs, share = cotangent.shape
    cap = pairs * 5 // (4 * N_EXP)
    rows_all = cap * N_EXP
    _, (wide_u, wide_z) = parts_of(half)
    count = 2 * len(PARTS)
    slots_u, slots_z = 2 * HIGH + 3, 2 * HIGH + 1
    bf16, dma = jnp.bfloat16, pltpu.SemaphoreType.DMA
    vmem, anywhere = pl.BlockSpec(memory_space=pltpu.VMEM), pl.BlockSpec(memory_space=pl.ANY)
    return pl.pallas_call(
        exchange_kernel,
        out_shape=(
            jax.ShapeDtypeStruct((rows, width), bf16),
            jax.ShapeDtypeStruct((rows_all, width), bf16),
            jax.ShapeDtypeStruct((rows_all, hidden), bf16),
        ),
        in_specs=[vmem, anywhere, vmem, vmem, vmem],
        out_specs=[vmem, anywhere, anywhere],
        scratch_shapes=[
            pltpu.VMEM((N_EXP, pairs), jnp.float32),
            pltpu.VMEM((1, pairs), jnp.float32),
            pltpu.VMEM((rows_all, share), bf16),
            pltpu.VMEM((2, 8, rows, half), bf16),
            pltpu.VMEM((2, 8, cap, half), bf16),
            pltpu.VMEM((rows_all, width), bf16),
            pltpu.VMEM((width, hidden), bf16),
            pltpu.VMEM((hidden, width), bf16),
            pltpu.VMEM((N_EXP, N_EXP, rows), bf16),
            pltpu.VMEM((rows_all, share), bf16),
            pltpu.VMEM((rows_all, share), bf16),
            pltpu.VMEM((rows_all, share), bf16),
            pltpu.VMEM((rows_all, share), bf16),
            pltpu.VMEM((rows_all, hidden), bf16),
            pltpu.VMEM((2, rows, half), jnp.float32),
            pltpu.VMEM((2, 8, cap, half), bf16),
            pltpu.VMEM((2, slots_u, rows, wide_u), bf16),
            pltpu.VMEM((2, slots_z, rows, wide_z), bf16),
            dma((count * N_EXP * 3,)), dma((count * N_EXP,)),
            dma((2 * N_EXP,)), dma((2 * N_EXP,)),
            dma((N_EXP,)), dma((N_EXP,)), dma((N_EXP,)), dma((N_EXP,)),
            dma((8,)), dma((8,)), dma((8,)), dma((8,)),
            dma((2 * N_EXP,)), dma((16,)), dma((count * N_EXP,)),
            dma((count * slots_u,)), dma((count * slots_z,)),
            dma((1,)), dma((N_EXP,)),
        ],
        compiler_params=pltpu.CompilerParams(
            collective_id=0, has_side_effects=True, vmem_limit_bytes=62 * 2**20
        ),
        name="exchange",
    )(tokens, weight, routes, combine, cotangent)


def weight_sum_kernel(x_ref, d_ref, o_ref):
    o_ref[...] = lax.dot_general(
        x_ref[...], d_ref[...], (((0,), (0,)), ((), ())), preferred_element_type=jnp.float32
    ).astype(o_ref.dtype)


def weight_sum(xc, dh):
    total, width = xc.shape
    hidden = dh.shape[1]
    return pl.pallas_call(
        weight_sum_kernel,
        out_shape=jax.ShapeDtypeStruct((width, hidden), jnp.bfloat16),
        grid=(width // 896,),
        in_specs=[
            pl.BlockSpec((total, 896), lambda i: (0, i)),
            pl.BlockSpec((total, hidden), lambda i: (0, 0)),
        ],
        out_specs=pl.BlockSpec((896, hidden), lambda i: (i, 0)),
        compiler_params=pltpu.CompilerParams(vmem_limit_bytes=62 * 2**20),
        name="weight_sum",
    )(xc, dh)


def local_dense(tokens, gate_weight, routes, combine, cotangent):
    pairs = routes.shape[0] * routes.shape[1]
    token_grad, xc, dh = exchange(
        tokens, gate_weight, routes.T, combine.T, cotangent.reshape(pairs, cotangent.shape[2])
    )
    grad = weight_sum(xc, dh)
    return (token_grad, grad[None])


def local(tokens, gate_weight, routes, combine, cotangent):
    dense = (
        lax.axis_size("expert") == N_EXP
        and lax.axis_size("replica") == 2
        and tokens.shape == (128, 3584)
        and gate_weight.shape[2] == 2 * cotangent.shape[2]
        and routes.shape[1] == 8
    )
    body = local_dense if dense else local_routed
    return body(tokens, gate_weight, routes, combine, cotangent)


def solution(mesh):
    return jax.shard_map(
        local,
        mesh=mesh,
        in_specs=(
            P("expert", "replica"),
            P("expert", "replica", None),
            P("expert", None),
            P("expert", None),
            P("expert", None, "replica"),
        ),
        out_specs=(P("expert", "replica"), P("expert", "replica", None)),
        check_vma=False,
    )
```
